32 devices in a mesh: fsdp: 4 (over y, x), seq: 8 (over z, core).
Axes of the slice: x: 2, y: 2, z: 4, core: 2. Of those that a mesh axis runs over, the one named last changes fastest.
Arguments:
- residual_in: bfloat16 [4, 1024, 2048], P('fsdp', 'seq'), may hold values from -6 to 6
- attn_gain: bfloat16 [2048], replicated, may hold values from 0.5 to 1.5
- mlp_gain: bfloat16 [2048], replicated, may hold values from 0.5 to 1.5
- w_qkv: bfloat16 [2048, 3, 2048], P('fsdp'), may hold values from -0.125 to 0.125
- w_out: bfloat16 [2048, 2048], P('fsdp'), may hold values from -1 to 1
- w_gate_up: bfloat16 [8192, 2, 2048], P('fsdp'), may hold values from -0.125 to 0.125
- w_down: bfloat16 [2048, 8192], P('fsdp'), may hold values from -0.0625 to 0.0625
- cotangent: bfloat16 [4, 1024, 2048], P('fsdp', 'seq'), may hold values from -6 to 6
Outputs:
- layer_out: bfloat16 [4, 1024, 2048], P('fsdp', 'seq')
- grad_input: float32 [4, 1024, 2048], P('fsdp', 'seq')
- grad_attn_gain: float32 [2048], P(('fsdp', 'seq'))
- grad_mlp_gain: float32 [2048], P(('fsdp', 'seq'))
- grad_qkv: float32 [2048, 3, 2048], P(('seq', 'fsdp'))
- grad_out_proj: float32 [2048, 2048], P(None, ('seq', 'fsdp'))
- grad_gate_up: float32 [8192, 2, 2048], P(('seq', 'fsdp'))
- grad_down: float32 [2048, 8192], P(None, ('seq', 'fsdp'))
The draws below stay inside these ranges and needn't reach their ends.
All inputs are finite; a program needn't handle non-finite values.
Results may differ from the reference program's by a relative error of at most 0.018.
Values may be sent and summed in bfloat16 or wider, within the bound.
No kernel may reach another device: no remote copies, remote signals or barrier semaphores. Data moves between devices by JAX's collectives and lax.ppermute only.
A program may use at most 384 MiB of HBM per device.

```python
import math
import jax
import jax.numpy as jnp
from jax import lax

D = 2048
HEADS = 32
HD = 64
FF = 8192
LEN = 1024
BATCH = 4


def strengthened(array, own_key, source, target, blocks, factor):
    owner, partner = [(jnp.arange(array.shape[axis_at]) // (array.shape[axis_at] // blocks)).reshape([-1 if axis == axis_at else 1 for axis in range(array.ndim)]) for axis_at in (source, target)]
    chosen = jax.random.permutation(own_key, blocks)[partner]
    strong = (owner == chosen) | (owner == (partner + blocks // 2) % blocks)
    return jnp.where(strong, factor * array, array)


def levels(own_key, shape, pieces, smallest, largest):
    def one(position, blocks):
        steps = jax.random.uniform(jax.random.fold_in(jax.random.fold_in(own_key, 6), position), (blocks,), jnp.float32, smallest / len(pieces), largest / len(pieces))
        return jnp.repeat(jnp.exp(steps), shape[position] // blocks).reshape((-1,) + (1,) * (len(shape) - position - 1))

    loudness = one(*pieces[0])
    for cut in pieces[1:]:
        loudness = loudness * one(*cut)
    return loudness


def scatter_about(own_key, dims, deviation, reach, pieces=(), kind=jnp.bfloat16):
    entries = jax.random.normal(own_key, dims, jnp.float32) * deviation
    if len(pieces) > 0:
        entries = levels(own_key, dims, pieces, -0.22, 0.18) * entries
    return jnp.clip(entries, min=-reach, max=reach).astype(kind)


def heavy_noise(stream_key, dims, deviation, bound, shards, heavy, held_as=jnp.bfloat16):
    entries = deviation * jax.random.normal(stream_key, dims, jnp.float32)
    if shards:
        entries = entries * levels(stream_key, dims, shards, -0.22, 0.18)
    return jnp.clip(strengthened(entries, jax.random.fold_in(stream_key, 3), *heavy), -bound, bound).astype(held_as)


def setup_inputs(seed: int = 0) -> dict:
    streams_of = jax.random.split(jax.random.key(seed), 9)
    return {
        "residual_in": scatter_about(streams_of[0], (BATCH, LEN, D), 1.0, 6.0, ((0, 4), (1, 8))),
        "attn_gain": jnp.clip(1.0 + 0.1 * jax.random.normal(streams_of[1], (D,), jnp.float32), 0.5, 1.5).astype(jnp.bfloat16),
        "mlp_gain": jnp.clip(1.0 + 0.1 * jax.random.normal(streams_of[2], (D,), jnp.float32), 0.5, 1.5).astype(jnp.bfloat16),
        "w_qkv": scatter_about(streams_of[3], (D, 3, D), D ** -0.5, 0.125, ((0, 4),)),
        "w_out": scatter_about(streams_of[4], (D, D), (max(1, D * 16 // LEN)) ** -0.5, 1.0, ((0, 4),)),
        "w_gate_up": scatter_about(streams_of[5], (FF, 2, D), D ** -0.5, 0.125, ((0, 4),)),
        "w_down": scatter_about(streams_of[6], (D, FF), FF ** -0.5, 0.0625, ((0, 4),)),
        "cotangent": heavy_noise(streams_of[7], (BATCH, LEN, D), 1.0, 6.0, ((0, 4), (1, 8)), (1, 2, 8, 2.0)),
    }


NORM_EPS = 1e-05
ROPE_BASE = 130000.0
HIGHEST_PRECISION = lax.Precision.HIGHEST

@jax.custom_vjp
def low(v):
    return lax.optimization_barrier(v.astype(jnp.bfloat16)).astype(jnp.float32)

@jax.custom_vjp
def low_back(v):
    return v

def low_keep(v):
    return (low(v), None)

def low_pass(kept, grad):
    return (grad,)

def back_keep(v):
    return (v, None)

def back_low(kept, grad):
    return (low(grad),)
low.defvjp(low_keep, low_pass)
low_back.defvjp(back_keep, back_low)

def rotate(matrix):
    shaped = matrix.reshape(matrix.shape[:-1] + (matrix.shape[-1] // HD, 2, HD // 2))
    turned = jnp.stack([-shaped[..., 1, :], shaped[..., 0, :]], axis=-2)
    return turned.reshape(matrix.shape)

def rope_tables(positions, columns):
    freq_index = (jnp.arange(columns, dtype=jnp.int32) % (HD // 2)).astype(jnp.float32)
    inverse = ROPE_BASE ** (-2.0 * freq_index / HD)
    angles = positions.astype(jnp.float32)[:, None] * inverse[None, :]
    return (jnp.cos(angles), jnp.sin(angles))

def rotary(matrix, cosine, sine_table):
    return matrix * cosine + rotate(matrix) * sine_table

def rms_norm(matrix, gain):
    return matrix * lax.rsqrt(lax.optimization_barrier(jnp.mean(matrix * matrix, axis=-1, keepdims=True)) + NORM_EPS) * gain

def attention(queries, key_rows, values):
    length = queries.shape[0]
    block_rows = min(512, length)
    inv_root = 1.0 / math.sqrt(HD)
    heads_q = queries.reshape(length // block_rows, block_rows, HEADS, HD)
    heads_k = key_rows.reshape(length, HEADS, HD)
    heads_v = values.reshape(length, HEADS, HD)
    offsets = jnp.arange(length // block_rows, dtype=jnp.int32) * block_rows
    key_pos = jnp.arange(length, dtype=jnp.int32)

    def one_block(operands):
        portion, offset = operands
        projected = jnp.einsum('qhd,khd->hqk', portion, heads_k, precision=HIGHEST_PRECISION) * inv_root
        scores = low_back(projected)
        query_pos = offset + jnp.arange(block_rows, dtype=jnp.int32)
        causal = key_pos[None, :] <= query_pos[:, None]
        exp_scores = jnp.exp(jnp.where(causal[None], scores, -10000.0))
        denominator = lax.optimization_barrier(jnp.sum(exp_scores, axis=-1))
        unnorm = low_back(jnp.einsum('hqk,khd->qhd', low(exp_scores), heads_v, precision=HIGHEST_PRECISION))
        return unnorm / jnp.transpose(denominator)[:, :, None]
    attended = lax.map(jax.checkpoint(one_block), (heads_q, offsets))
    return attended.reshape(length, HEADS * HD)

def decoder(inputs, attn_gain, mlp_gain, w_qkv, w_out, w_gate_up, w_down):
    length = inputs.shape[0]
    cosine, sine_table = rope_tables(jnp.arange(length, dtype=jnp.int32), inputs.shape[1])
    normed_one = low(rms_norm(inputs, attn_gain))
    projected = jnp.einsum('td,fpd->ptf', normed_one, w_qkv, precision=HIGHEST_PRECISION)
    queries = low(rotary(low_back(projected[0]), cosine, sine_table))
    key_rows = low(rotary(low_back(projected[1]), cosine, sine_table))
    values = low(low_back(projected[2]))
    attended = low(low_back(attention(queries, key_rows, values)))
    branch = low_back(jnp.einsum('ti,fi->tf', attended, w_out, precision=HIGHEST_PRECISION))
    residual = inputs + branch
    normed_two = low(rms_norm(residual, mlp_gain))
    gate_up = low_back(jnp.einsum('td,jpd->ptj', normed_two, w_gate_up, precision=HIGHEST_PRECISION))
    hidden = low(jax.nn.silu(gate_up[0]) * gate_up[1])
    return residual + jnp.einsum('tj,fj->tf', hidden, w_down, precision=HIGHEST_PRECISION)

def reference(residual_in, attn_gain, mlp_gain, w_qkv, w_out, w_gate_up, w_down, cotangent):
    weights = (attn_gain.astype(jnp.float32), mlp_gain.astype(jnp.float32), w_qkv.astype(jnp.float32), w_out.astype(jnp.float32), w_gate_up.astype(jnp.float32), w_down.astype(jnp.float32))
    initial = tuple((jnp.zeros(weight.shape, jnp.float32) for weight in weights))

    def advance(running, sequence):
        seq_input, seq_grad = sequence
        result, pullback = jax.vjp(decoder, seq_input.astype(jnp.float32), weights[0], weights[1], weights[2], weights[3], weights[4], weights[5])
        gradients = pullback(seq_grad.astype(jnp.float32))
        running = tuple((total_now + part_now for total_now, part_now in zip(running, gradients[1:])))
        return (running, (result.astype(jnp.bfloat16), gradients[0]))
    totals, (outputs, grad_input) = lax.scan(advance, initial, (residual_in, cotangent))
    return (outputs, grad_input, totals[0], totals[1], totals[2], totals[3], totals[4], totals[5])
```

```python
import functools
import math

import jax
import jax.numpy as jnp
from jax import lax
from jax.experimental import pallas as pl
from jax.experimental.pallas import tpu as pltpu
from jax.sharding import Mesh
from jax.sharding import PartitionSpec as P

HD = 64


NORM_EPS = 1e-05
ROPE_BASE = 130000.0


def rotate(matrix):
    shaped = matrix.reshape(matrix.shape[:-1] + (matrix.shape[-1] // HD, 2, HD // 2))
    turned = jnp.stack([-shaped[..., 1, :], shaped[..., 0, :]], axis=-2)
    return turned.reshape(matrix.shape)


def rotate_back(matrix):
    shaped = matrix.reshape(matrix.shape[:-1] + (matrix.shape[-1] // HD, 2, HD // 2))
    turned = jnp.stack([shaped[..., 1, :], -shaped[..., 0, :]], axis=-2)
    return turned.reshape(matrix.shape)


def rope_tables(positions, columns):
    freq_index = (jnp.arange(columns, dtype=jnp.int32) % (HD // 2)).astype(jnp.float32)
    inverse = ROPE_BASE ** (-2.0 * freq_index / HD)
    angles = positions.astype(jnp.float32)[:, None] * inverse[None, :]
    return (jnp.cos(angles), jnp.sin(angles))


def rms_scale(matrix):
    return lax.rsqrt(jnp.mean(matrix * matrix, axis=-1, keepdims=True) + NORM_EPS)


def rms_back(grad_normed, matrix, scale_rows, gain):
    weighted = grad_normed * gain
    inner_mean = jnp.mean(weighted * matrix, axis=-1, keepdims=True)
    grad_matrix = scale_rows * weighted - matrix * scale_rows**3 * inner_mean
    grad_gain = jnp.sum(grad_normed * matrix * scale_rows, axis=0)
    return (grad_matrix, grad_gain)


def attend_forward(queries, key_rows, values):
    seq_count, length, width_here = queries.shape
    heads_here = width_here // HD
    q_block = min(512, length)
    k_block = min(256, length)
    inv_root = 1.0 / math.sqrt(HD)
    shaped_q = queries.reshape(seq_count, length, heads_here, HD)
    shaped_k = key_rows.reshape(seq_count, length, heads_here, HD)
    shaped_v = values.reshape(seq_count, length, heads_here, HD)

    def query_step(q_index, carried):
        attended, totals = carried
        offset = q_index * q_block
        q_rows = lax.dynamic_slice_in_dim(shaped_q, offset, q_block, 1)
        query_pos = offset + jnp.arange(q_block, dtype=jnp.int32)

        def key_step(k_index, running):
            unnorm, denominator = running
            k_start = k_index * k_block
            k_rows = lax.dynamic_slice_in_dim(shaped_k, k_start, k_block, 1)
            v_rows = lax.dynamic_slice_in_dim(shaped_v, k_start, k_block, 1)
            scores = (
                jnp.einsum("bqhd,bkhd->bhqk", q_rows, k_rows, preferred_element_type=jnp.float32)
                * inv_root
            )
            causal = (k_start + jnp.arange(k_block, dtype=jnp.int32))[None, :] <= query_pos[:, None]
            exp_scores = jnp.where(causal, jnp.exp(scores), 0.0)
            denominator = denominator + jnp.sum(exp_scores, axis=-1)
            unnorm = unnorm + jnp.einsum(
                "bhqk,bkhd->bqhd",
                exp_scores.astype(jnp.bfloat16),
                v_rows,
                preferred_element_type=jnp.float32,
            )
            return (unnorm, denominator)

        start_state = (
            jnp.zeros((seq_count, q_block, heads_here, HD), jnp.float32),
            jnp.zeros((seq_count, heads_here, q_block), jnp.float32),
        )
        unnorm, denominator = lax.fori_loop(0, (offset + q_block) // k_block, key_step, start_state)
        block_out = unnorm / jnp.transpose(denominator, (0, 2, 1))[..., None]
        attended = lax.dynamic_update_slice_in_dim(attended, block_out, offset, 1)
        totals = lax.dynamic_update_slice_in_dim(totals, denominator, offset, 2)
        return (attended, totals)

    initial = (
        jnp.zeros((seq_count, length, heads_here, HD), jnp.float32),
        jnp.zeros((seq_count, heads_here, length), jnp.float32),
    )
    attended, totals = lax.fori_loop(0, length // q_block, query_step, initial)
    return (attended.reshape(seq_count, length, width_here), totals)


def attend_backward(queries, key_rows, values, attended, totals, grad_attended):
    seq_count, length, width_here = queries.shape
    heads_here = width_here // HD
    q_block = min(512, length)
    k_block = min(256, length)
    inv_root = 1.0 / math.sqrt(HD)
    shaped_q = queries.reshape(seq_count, length, heads_here, HD)
    shaped_k = key_rows.reshape(seq_count, length, heads_here, HD)
    shaped_v = values.reshape(seq_count, length, heads_here, HD)
    shaped_grad = grad_attended.reshape(seq_count, length, heads_here, HD).astype(jnp.float32)
    shaped_att = attended.reshape(seq_count, length, heads_here, HD)
    totals_rows = jnp.transpose(totals, (0, 2, 1))
    grad_total = -jnp.sum(shaped_grad * shaped_att, axis=-1) / totals_rows
    grad_unnorm = (shaped_grad / totals_rows[..., None]).astype(jnp.bfloat16)

    def query_step(q_index, carried):
        grad_q, grad_k, grad_v = carried
        offset = q_index * q_block
        q_rows = lax.dynamic_slice_in_dim(shaped_q, offset, q_block, 1)
        g_rows = lax.dynamic_slice_in_dim(grad_unnorm, offset, q_block, 1)
        total_rows = jnp.transpose(
            lax.dynamic_slice_in_dim(grad_total, offset, q_block, 1), (0, 2, 1)
        )
        query_pos = offset + jnp.arange(q_block, dtype=jnp.int32)

        def key_step(k_index, running):
            dq_acc, dk_all, dv_all = running
            k_start = k_index * k_block
            k_rows = lax.dynamic_slice_in_dim(shaped_k, k_start, k_block, 1)
            v_rows = lax.dynamic_slice_in_dim(shaped_v, k_start, k_block, 1)
            scores = (
                jnp.einsum("bqhd,bkhd->bhqk", q_rows, k_rows, preferred_element_type=jnp.float32)
                * inv_root
            )
            causal = (k_start + jnp.arange(k_block, dtype=jnp.int32))[None, :] <= query_pos[:, None]
            exp_scores = jnp.where(causal, jnp.exp(scores), 0.0)
            grad_prob = jnp.einsum(
                "bqhd,bkhd->bhqk", g_rows, v_rows, preferred_element_type=jnp.float32
            )
            grad_scores = (exp_scores * (grad_prob + total_rows[..., None])).astype(jnp.bfloat16)
            dq_acc = (
                dq_acc
                + jnp.einsum(
                    "bhqk,bkhd->bqhd", grad_scores, k_rows, preferred_element_type=jnp.float32
                )
                * inv_root
            )
            dk_part = (
                jnp.einsum(
                    "bhqk,bqhd->bkhd", grad_scores, q_rows, preferred_element_type=jnp.float32
                )
                * inv_root
            )
            dv_part = jnp.einsum(
                "bhqk,bqhd->bkhd",
                exp_scores.astype(jnp.bfloat16),
                g_rows,
                preferred_element_type=jnp.float32,
            )
            dk_slice = lax.dynamic_slice_in_dim(dk_all, k_start, k_block, 1) + dk_part
            dv_slice = lax.dynamic_slice_in_dim(dv_all, k_start, k_block, 1) + dv_part
            dk_all = lax.dynamic_update_slice_in_dim(dk_all, dk_slice, k_start, 1)
            dv_all = lax.dynamic_update_slice_in_dim(dv_all, dv_slice, k_start, 1)
            return (dq_acc, dk_all, dv_all)

        start_state = (jnp.zeros((seq_count, q_block, heads_here, HD), jnp.float32), grad_k, grad_v)
        dq_block, grad_k, grad_v = lax.fori_loop(
            0, (offset + q_block) // k_block, key_step, start_state
        )
        grad_q = lax.dynamic_update_slice_in_dim(grad_q, dq_block, offset, 1)
        return (grad_q, grad_k, grad_v)

    empty = jnp.zeros((seq_count, length, heads_here, HD), jnp.float32)
    grad_q, grad_k, grad_v = lax.fori_loop(0, length // q_block, query_step, (empty, empty, empty))
    cosine, sine_table = rope_tables(jnp.arange(length, dtype=jnp.int32), width_here)
    grad_q = grad_q.reshape(seq_count, length, width_here)
    grad_k = grad_k.reshape(seq_count, length, width_here)
    grad_v = grad_v.reshape(seq_count, length, width_here)
    raw_q = grad_q * cosine + rotate_back(grad_q * sine_table)
    raw_k = grad_k * cosine + rotate_back(grad_k * sine_table)
    return jnp.stack([raw_q, raw_k, grad_v]).astype(jnp.bfloat16)


def general_body(residual_in, attn_gain, mlp_gain, w_qkv, w_out, w_gate_up, w_down, cotangent):
    seq_count, shard_len, model_width = residual_in.shape
    tokens = seq_count * shard_len
    seq_index = lax.axis_index("seq")
    positions = seq_index * shard_len + jnp.arange(tokens, dtype=jnp.int32) % shard_len
    cosine, sine_table = rope_tables(positions, model_width)
    inputs = residual_in.reshape(tokens, model_width).astype(jnp.float32)
    gain_one = attn_gain.astype(jnp.float32)
    gain_two = mlp_gain.astype(jnp.float32)
    scale_one = rms_scale(inputs)
    normed_one = (inputs * scale_one * gain_one).astype(jnp.bfloat16)
    qkv_full, out_full = (
        lax.all_gather(w_qkv, "fsdp", axis=0, tiled=True),
        lax.all_gather(w_out, "fsdp", axis=0, tiled=True),
    )
    projected = jnp.einsum("td,fpd->ptf", normed_one, qkv_full, preferred_element_type=jnp.float32)
    queries = (projected[0] * cosine + rotate(projected[0]) * sine_table).astype(jnp.bfloat16)
    key_rows = (projected[1] * cosine + rotate(projected[1]) * sine_table).astype(jnp.bfloat16)
    values = projected[2].astype(jnp.bfloat16)
    stacked = jnp.stack([queries, key_rows, values]).reshape(3, seq_count, shard_len, model_width)
    head_view = lax.all_to_all(stacked, "seq", split_axis=3, concat_axis=2, tiled=True)
    attended, totals = attend_forward(head_view[0], head_view[1], head_view[2])
    attended_heads = attended.astype(jnp.bfloat16)
    sent_back = lax.all_to_all(attended_heads, "seq", split_axis=1, concat_axis=2, tiled=True)
    attended_low = sent_back.reshape(tokens, model_width)
    branch = jnp.einsum("ti,fi->tf", attended_low, out_full, preferred_element_type=jnp.float32)
    residual = inputs + branch
    scale_two = rms_scale(residual)
    normed_two = (residual * scale_two * gain_two).astype(jnp.bfloat16)
    up_full, down_full = (
        lax.all_gather(w_gate_up, "fsdp", axis=0, tiled=True),
        lax.all_gather(w_down, "fsdp", axis=0, tiled=True),
    )
    gate_up = jnp.einsum("td,jpd->ptj", normed_two, up_full, preferred_element_type=jnp.float32)
    hidden = (jax.nn.silu(gate_up[0]) * gate_up[1]).astype(jnp.bfloat16)
    mlp_term = jnp.einsum("tj,fj->tf", hidden, down_full, preferred_element_type=jnp.float32)
    layer_out = (
        (residual + mlp_term).astype(jnp.bfloat16).reshape(seq_count, shard_len, model_width)
    )
    grad_out = cotangent.reshape(tokens, model_width)
    up_again, down_again = (
        lax.all_gather(w_gate_up, "fsdp", axis=0, tiled=True),
        lax.all_gather(w_down, "fsdp", axis=0, tiled=True),
    )
    grad_hidden = jnp.einsum("tf,fj->tj", grad_out, down_again, preferred_element_type=jnp.float32)
    sigmoid_gate = jax.nn.sigmoid(gate_up[0])
    grad_gate = grad_hidden * gate_up[1] * sigmoid_gate * (1.0 + gate_up[0] * (1.0 - sigmoid_gate))
    grad_up = grad_hidden * jax.nn.silu(gate_up[0])
    grad_gu = jnp.stack([grad_gate, grad_up]).astype(jnp.bfloat16)
    grad_normed_two = jnp.einsum(
        "ptj,jpd->td", grad_gu, up_again, preferred_element_type=jnp.float32
    )
    ff_width = grad_gu.shape[2]
    unit_rows = jnp.concatenate([grad_gu, hidden[None]], axis=0).reshape(
        3, seq_count, shard_len, ff_width
    )
    unit_cols = lax.all_to_all(unit_rows, "seq", split_axis=3, concat_axis=2, tiled=True)
    normed_piece = lax.all_gather(
        normed_two.reshape(seq_count, shard_len, model_width), "seq", axis=1, tiled=True
    )
    grad_piece = lax.all_gather(cotangent, "seq", axis=1, tiled=True)
    gu_part = jnp.einsum(
        "psnj,snd->jpd", unit_cols[:2], normed_piece, preferred_element_type=jnp.float32
    )
    down_part = jnp.einsum(
        "snf,snj->fj", grad_piece, unit_cols[2], preferred_element_type=jnp.float32
    )
    gu_part, down_part = (gu_part, down_part)
    grad_gate_up, grad_down = (
        lax.psum_scatter(
            gu_part.astype(jnp.bfloat16), "fsdp", scatter_dimension=0, tiled=True
        ).astype(jnp.float32),
        lax.psum_scatter(
            down_part.astype(jnp.bfloat16), "fsdp", scatter_dimension=1, tiled=True
        ).astype(jnp.float32),
    )
    grad_norm_two, grad_gain_two = rms_back(grad_normed_two, residual, scale_two, gain_two)
    grad_residual = grad_out.astype(jnp.float32) + grad_norm_two
    qkv_back, out_back = (
        lax.all_gather(w_qkv, "fsdp", axis=0, tiled=True),
        lax.all_gather(w_out, "fsdp", axis=0, tiled=True),
    )
    grad_branch = grad_residual.astype(jnp.bfloat16)
    grad_attended = jnp.einsum(
        "tf,fi->ti", grad_branch, out_back, preferred_element_type=jnp.float32
    )
    grad_attended = grad_attended.astype(jnp.bfloat16).reshape(seq_count, shard_len, model_width)
    grad_heads = lax.all_to_all(grad_attended, "seq", split_axis=2, concat_axis=1, tiled=True)
    grad_stacked = attend_backward(
        head_view[0], head_view[1], head_view[2], attended, totals, grad_heads
    )
    normed_piece = lax.all_gather(
        normed_one.reshape(seq_count, shard_len, model_width), "seq", axis=1, tiled=True
    )
    branch_piece = lax.all_gather(
        grad_branch.reshape(seq_count, shard_len, model_width), "seq", axis=1, tiled=True
    )
    grad_piece = grad_stacked
    qkv_part = jnp.einsum(
        "psnf,snd->fpd", grad_piece, normed_piece, preferred_element_type=jnp.float32
    )
    out_part = jnp.einsum(
        "snf,sni->fi", branch_piece, attended_heads, preferred_element_type=jnp.float32
    )
    qkv_part, out_part = (qkv_part, out_part)
    grad_qkv, grad_out_proj = (
        lax.psum_scatter(
            qkv_part.astype(jnp.bfloat16), "fsdp", scatter_dimension=0, tiled=True
        ).astype(jnp.float32),
        lax.psum_scatter(
            out_part.astype(jnp.bfloat16), "fsdp", scatter_dimension=1, tiled=True
        ).astype(jnp.float32),
    )
    grad_projected = lax.all_to_all(grad_stacked, "seq", split_axis=2, concat_axis=3, tiled=True)
    grad_projected = grad_projected.reshape(3, tokens, model_width)
    grad_normed_one = jnp.einsum(
        "ptf,fpd->td", grad_projected, qkv_back, preferred_element_type=jnp.float32
    )
    grad_norm_one, grad_gain_one = rms_back(grad_normed_one, inputs, scale_one, gain_one)
    grad_input = (grad_residual + grad_norm_one).reshape(seq_count, shard_len, model_width)
    grad_attn_gain, grad_mlp_gain = (
        lax.psum_scatter(grad_gain_one, ("fsdp", "seq"), scatter_dimension=0, tiled=True),
        lax.psum_scatter(grad_gain_two, ("fsdp", "seq"), scatter_dimension=0, tiled=True),
    )
    return (
        layer_out,
        grad_input,
        grad_attn_gain,
        grad_mlp_gain,
        grad_qkv,
        grad_out_proj,
        grad_gate_up,
        grad_down,
    )


def general_solution(mesh):
    return jax.shard_map(
        general_body,
        mesh=mesh,
        in_specs=(
            P("fsdp", "seq", None),
            P(),
            P(),
            P("fsdp", None, None),
            P("fsdp", None),
            P("fsdp", None, None),
            P("fsdp", None),
            P("fsdp", "seq", None),
        ),
        out_specs=(
            P("fsdp", "seq", None),
            P("fsdp", "seq", None),
            P(("fsdp", "seq")),
            P(("fsdp", "seq")),
            P(("seq", "fsdp"), None, None),
            P(None, ("seq", "fsdp")),
            P(("seq", "fsdp"), None, None),
            P(None, ("seq", "fsdp")),
        ),
        check_vma=False,
    )


BF = jnp.bfloat16
F32 = jnp.float32
AXES = ("y", "x", "z", "c")
PAIR = [(0, 1), (1, 0)]
BLK = 128
ORDER = (0, 1, 3, 2)
Q_ROWS = 256


def swap(value, axis):
    return lax.ppermute(value, axis, PAIR)


def hop(value, dist):
    return lax.ppermute(value, "z", [(i, i ^ dist) for i in range(4)])


def tick(*values):
    return lax.optimization_barrier(values)


def with_partner(held, other):
    both = jnp.concatenate([held, other], axis=0)
    return jnp.concatenate([both, swap(both, "c")], axis=0)


def fold_core(part):
    n = part.shape[0] // 2
    return part[:n].astype(F32) + swap(part[n:].astype(BF), "c").astype(F32)


def fold_plane(kept, plane):
    n = kept.shape[0] // 2
    return kept[:n] + swap(kept[n:].astype(BF), plane).astype(F32)


def fold_hops(parts):
    total = parts[0]
    for j, part in zip(ORDER[1:], parts[1:]):
        total = total + hop(part.astype(BF), j).astype(F32)
    return total


def send_core(pieces):
    return jnp.stack([pieces[:, 0], swap(pieces[:, 1], "c")], axis=1)


def send_plane(pieces, plane):
    return jnp.stack([pieces[:, :, 0], swap(pieces[:, :, 1], plane)], axis=2)


def send_hops(pieces):
    return jnp.stack([hop(pieces[i], j) if j else pieces[i] for i, j in enumerate(ORDER)])


def turn(value, back):
    lane = lax.broadcasted_iota(jnp.int32, value.shape, 1) % HD
    up = pltpu.roll(value, HD // 2, 1)
    down = pltpu.roll(value, value.shape[1] - HD // 2, 1)
    return jnp.where(lane < HD // 2, down, -up) if back else jnp.where(lane < HD // 2, -down, up)


def head_mask(value, head):
    lane = lax.broadcasted_iota(jnp.int32, value.shape, 1)
    return jnp.where((lane < HD) == (head == 0), value, jnp.zeros_like(value))


def dot(left, right, left_dim, right_dim):
    return lax.dot_general(
        left, right, (((left_dim,), (right_dim,)), ((), ())), preferred_element_type=F32
    )


def causal_exp(scores, start):
    rows, cols = scores.shape
    query = start + lax.broadcasted_iota(jnp.int32, (rows, rows), 0)
    key = cols - rows + lax.broadcasted_iota(jnp.int32, (rows, rows), 1)
    last = jnp.where(key <= query, jnp.exp(scores[:, cols - rows :]), 0.0)
    if cols == rows:
        return last
    return jnp.concatenate([jnp.exp(scores[:, : cols - rows]), last], axis=1)


def chunk_of(slot):
    dist = slot >> 1
    return dist ^ (dist >> 1)


def attend_kernel(place, proj, cosine, sine, q_out, k_out, v_out, att_out, den_out, low_out):
    length = q_out.shape[1]
    me = place[0]
    for block in range(length // BLK):
        slot = me ^ block
        here = proj[chunk_of(slot), slot & 1, 0]
        rows = slice(block * BLK, (block + 1) * BLK)
        cos_rows, sin_rows = cosine[rows, :], sine[rows, :]
        raw_q, raw_k = here[:, :128], here[:, 128:256]
        q_out[0, rows, :] = (raw_q * cos_rows + turn(raw_q, False) * sin_rows).astype(BF)
        k_out[0, rows, :] = (raw_k * cos_rows + turn(raw_k, False) * sin_rows).astype(BF)
        v_out[0, rows, :] = here[:, 256:].astype(BF)
    for start in range(0, length, Q_ROWS):
        seen = start + Q_ROWS
        queries = q_out[0, start:seen, :] * jnp.asarray(0.125, BF)
        keys, values = k_out[0, :seen, :], v_out[0, :seen, :]
        unnorm, den = None, None
        for head in range(2):
            exp_scores = causal_exp(dot(head_mask(queries, head), keys, 1, 1), start)
            total = jnp.sum(exp_scores, axis=1, keepdims=True)
            part = dot(exp_scores.astype(BF), head_mask(values, head), 1, 0)
            total = head_mask(jnp.broadcast_to(total, part.shape), head)
            unnorm = part if unnorm is None else unnorm + part
            den = total if den is None else den + total
        attended = unnorm / den
        att_out[0, start:seen, :] = attended
        den_out[0, start:seen, :] = den
        for block in range(start // BLK, seen // BLK):
            slot = me ^ block
            first = block * BLK - start
            low_out[chunk_of(slot), slot & 1, 0] = attended[first : first + BLK].astype(BF)


def attend_back_kernel(
    place, q_ref, k_ref, v_ref, att_ref, den_ref, grad_ref, cosine, sine, out, grad, grad_q, grad_k, grad_v
):
    length = q_ref.shape[1]
    me = place[0]
    for block in range(length // BLK):
        slot = me ^ block
        grad[block * BLK : (block + 1) * BLK, :] = grad_ref[chunk_of(slot), slot & 1, 0].astype(F32)
    grad_k[...] = jnp.zeros_like(grad_k)
    grad_v[...] = jnp.zeros_like(grad_v)
    for start in range(0, length, Q_ROWS):
        seen = start + Q_ROWS
        queries = q_ref[0, start:seen, :] * jnp.asarray(0.125, BF)
        keys, values = k_ref[0, :seen, :], v_ref[0, :seen, :]
        grad_rows, den = grad[start:seen, :], den_ref[0, start:seen, :]
        unnorm = (grad_rows / den).astype(BF)
        weighted = grad_rows * att_ref[0, start:seen, :] / den
        total_q = None
        for head in range(2):
            q_head, g_head = head_mask(queries, head), head_mask(unnorm, head)
            exp_scores = causal_exp(dot(q_head, keys, 1, 1), start)
            grad_total = -jnp.sum(head_mask(weighted, head), axis=1, keepdims=True)
            grad_scores = (exp_scores * (dot(g_head, values, 1, 1) + grad_total)).astype(BF)
            part = dot(grad_scores, head_mask(keys, head), 1, 0)
            total_q = part if total_q is None else total_q + part
            grad_k[:seen, :] += dot(grad_scores, q_head, 0, 0)
            grad_v[:seen, :] += dot(exp_scores.astype(BF), g_head, 0, 0)
        grad_q[start:seen, :] = total_q * 0.125
    for block in range(length // BLK):
        slot = me ^ block
        rows = slice(block * BLK, (block + 1) * BLK)
        cos_rows, sin_rows = cosine[rows, :], sine[rows, :]
        for part, held in enumerate((grad_q, grad_k)):
            value = held[rows, :]
            raw = value * cos_rows + turn(value * sin_rows, True)
            out[chunk_of(slot), slot & 1, 0, :, part * 128 : (part + 1) * 128] = raw.astype(BF)
        out[chunk_of(slot), slot & 1, 0, :, 256:] = grad_v[rows, :].astype(BF)


def whole(shape):
    return pl.BlockSpec(shape, lambda i, place: (0,) * len(shape))


def per_seq(shape, at):
    return pl.BlockSpec(shape, lambda i, place: tuple(i if d == at else 0 for d in range(len(shape))))


def attend(place, proj, cosine, sine):
    length = cosine.shape[0]
    seq = jax.ShapeDtypeStruct((2, length, 128), BF)
    wide = jax.ShapeDtypeStruct((2, length, 128), F32)
    return pl.pallas_call(
        attend_kernel,
        grid_spec=pltpu.PrefetchScalarGridSpec(
            num_scalar_prefetch=1,
            grid=(2,),
            in_specs=[per_seq((4, 2, 1, BLK, 384), 2), whole((length, 128)), whole((length, 128))],
            out_specs=[per_seq((1, length, 128), 0)] * 5 + [per_seq((4, 2, 1, BLK, 128), 2)],
        ),
        out_shape=[seq, seq, seq, wide, wide, jax.ShapeDtypeStruct((4, 2, 2, BLK, 128), BF)],
        compiler_params=pltpu.CompilerParams(vmem_limit_bytes=40 << 20),
        cost_estimate=pl.CostEstimate(flops=4 * 10**9, bytes_accessed=8 << 20, transcendentals=4 << 20),
        name="attend",
    )(place, proj, cosine, sine)


def attend_back(place, saved, grad_slots, cosine, sine):
    length = cosine.shape[0]
    return pl.pallas_call(
        attend_back_kernel,
        grid_spec=pltpu.PrefetchScalarGridSpec(
            num_scalar_prefetch=1,
            grid=(2,),
            in_specs=[per_seq((1, length, 128), 0)] * 5
            + [per_seq((4, 2, 1, BLK, 128), 2), whole((length, 128)), whole((length, 128))],
            out_specs=per_seq((4, 2, 1, BLK, 384), 2),
            scratch_shapes=[pltpu.VMEM((length, 128), F32)] * 4,
        ),
        out_shape=jax.ShapeDtypeStruct((4, 2, 2, BLK, 384), BF),
        compiler_params=pltpu.CompilerParams(vmem_limit_bytes=40 << 20),
        cost_estimate=pl.CostEstimate(flops=10 * 10**9, bytes_accessed=8 << 20, transcendentals=4 << 20),
        name="attend_back",
    )(place, *saved, grad_slots, cosine, sine)


def perm_of(target):
    pairs = []
    for index in range(32):
        bits = [(index >> shift) & 1 for shift in (4, 3, 2, 1, 0)]
        place = 0
        for bit in target(*bits):
            place = 2 * place + bit
        pairs.append((index, place))
    return pairs


def assemble(pieces, shape):
    total = jnp.zeros(shape, pieces[0][0].dtype)
    for piece, row, col in pieces:
        total = lax.dynamic_update_slice(total, piece, (row, col))
    return total


def slot_of(rel):
    bit_y, bit_z0, bit_c, bit_z1 = rel >> 3, (rel >> 2) & 1, (rel >> 1) & 1, rel & 1
    return ORDER.index(2 * bit_z1 + bit_z0) * 4 + bit_c * 2 + bit_y


def to_heads_kernel(place, slots, out):
    for rel in range(16):
        pair = place[1] ^ rel
        out[:, pl.ds(pl.multiple_of(pair * 128, 128), 128)] = slots[slot_of(rel)]


def to_slots_kernel(place, rows, out):
    for rel in range(16):
        pair = place[1] ^ rel
        out[slot_of(rel)] = rows[:, pl.ds(pl.multiple_of(pair * 128, 128), 128)]


def reorder(kernel, place, value, shape):
    return pl.pallas_call(
        kernel,
        in_specs=[pl.BlockSpec(memory_space=pltpu.SMEM), pl.BlockSpec(memory_space=pltpu.VMEM)],
        out_specs=pl.BlockSpec(memory_space=pltpu.VMEM),
        out_shape=jax.ShapeDtypeStruct(shape, BF),
        cost_estimate=pl.CostEstimate(flops=0, bytes_accessed=1 << 20, transcendentals=0),
        name=kernel.__name__,
    )(place, value)


def split(value, dim, bit):
    size = value.shape[dim] // 2
    return (
        lax.dynamic_slice_in_dim(value, bit * size, size, dim),
        lax.dynamic_slice_in_dim(value, (1 - bit) * size, size, dim),
    )


def ff_place(at_y, at_x, at_z1, at_z0, at_c):
    return at_y, at_z0, at_z1, at_x, at_c


def attn_place(at_y, at_x, at_z1, at_z0, at_c):
    return at_z1, at_x, at_y, at_z0, at_c


def move(value, target):
    return lax.ppermute(value.astype(BF), AXES, perm_of(target)).astype(F32)


def body(residual_in, attn_gain, mlp_gain, w_qkv, w_out, w_gate_up, w_down, cotangent):
    y, x, z, c = [lax.axis_index(name) for name in AXES]
    z1, z0 = z >> 1, z & 1
    group, part = 2 * y + x, 2 * z + c
    width = residual_in.shape[2]
    length = BLK * 8
    quarter = 4 * BLK
    units = w_gate_up.shape[0] // 8
    inputs = residual_in[0].astype(F32)
    gain_one, gain_two = attn_gain.astype(F32), mlp_gain.astype(F32)
    scale_one = rms_scale(inputs)
    normed_one = (inputs * scale_one * gain_one).astype(BF)

    qkv_sent = lax.dynamic_slice_in_dim(w_qkv, (4 * c + 2 * z1) * HD, 2 * HD, 0)
    qkv_sent = jnp.transpose(qkv_sent, (1, 0, 2)).reshape(3 * 2 * HD, width)
    x_pairs = [((i & 1) * 4 + i, (1 - (i & 1)) * 4 + i) for i in range(4)]
    y_pairs = [((i >> 1) * 4 + i, (1 - (i >> 1)) * 4 + i) for i in range(4)]
    hops = [normed_one] + [hop(normed_one, j) for j in ORDER[1:]]
    others = [swap(normed_one, "y")]
    qkv_moved = lax.ppermute(qkv_sent, ("x", "z"), x_pairs)
    rows, cols = w_out.shape[0], width // 2
    out_own = lax.dynamic_slice_in_dim(w_out, c * cols, cols, 1)
    others[0], out_own = tick(others[0], out_own)
    out_y = swap(out_own, "y")
    for held in hops[1:]:
        others.append(swap(held, "y"))
    out_pair, _ = tick(jnp.concatenate([out_own, out_y], axis=0), hops[3])
    out_x = swap(out_pair, "x")
    normed_all = jnp.concatenate([with_partner(*item) for item in zip(hops, others)], axis=0)
    heads_qkv = jnp.where(x == z0, qkv_sent, qkv_moved)

    def columns(side):
        first = (8 * (2 * z1 + side) + 4 * c + z0) * units
        return jnp.concatenate(
            [lax.dynamic_slice_in_dim(w_down, first + 2 * j * units, units, 1) for j in range(2)], axis=1
        )

    gu_sent = [lax.dynamic_slice_in_dim(w_gate_up, (4 * c + 2 * j + z0) * units, units, 0) for j in range(2)]
    gu_sent = jnp.transpose(jnp.stack(gu_sent), (2, 0, 1, 3)).reshape(2, 2 * units, width)
    down_own, down_sent = columns(x), columns(1 - x)

    normed_all, cot, gate_sent = tick(normed_all, cotangent[0], gu_sent[0])
    cot_hops = [cot] + [hop(cot, j) for j in ORDER[1:]]
    gate_moved = lax.ppermute(gate_sent, ("y", "z"), y_pairs)

    cos_half, sin_half = rope_tables(jnp.arange(length, dtype=jnp.int32), HD // 2)
    cosine, sine = jnp.tile(cos_half, (1, 4)), jnp.tile(sin_half, (1, 4))
    place = jnp.stack([part, 8 * y + 4 * z0 + 2 * c + z1]).astype(jnp.int32)
    proj = dot(normed_all, heads_qkv, 1, 1)
    *saved, low_slots = attend(place, proj.reshape(4, 2, 2, BLK, 384), cosine, sine)
    pieces = send_plane(send_core(low_slots), "y")
    pieces, out_x, down_sent, cot = tick(pieces, out_x, down_sent, cot)
    pieces = send_hops(pieces)
    out_half = jnp.concatenate([out_pair, out_x], axis=0)
    out_c = swap(out_half, "c")
    cot_others = [swap(cot, "x")]
    down_x = swap(down_sent, "x")
    out_full = assemble(
        [
            (block[i * rows : (i + 1) * rows], (group ^ flip) * rows, side * cols)
            for block, side in ((out_half, c), (out_c, 1 - c))
            for i, flip in enumerate((0, 2, 1, 3))
        ],
        (width, width),
    )
    attended = reorder(to_heads_kernel, place, pieces.reshape(16, BLK, 128), (BLK, width))
    residual = inputs + dot(attended, out_full, 1, 1)
    scale_two = rms_scale(residual)
    normed_two = (residual * scale_two * gain_two).astype(BF)

    normed_two, *moved = tick(
        normed_two, cot_others[0], *cot_hops[1:], down_x, gate_moved, gu_sent[1], down_own
    )
    cot_others[0], cot_hops[1:], (down_x, gate_moved, up_sent, down_own) = moved[0], moved[1:4], moved[4:]
    hops = [normed_two] + [hop(normed_two, j) for j in ORDER[1:]]
    others = [swap(normed_two, "x")]
    cot_others.append(swap(cot_hops[1], "x"))
    up_moved = lax.ppermute(up_sent, ("y", "z"), y_pairs)
    down_pair = jnp.concatenate([down_own, down_x], axis=0)
    down_y = swap(down_pair, "y")
    for i in (1, 2, 3):
        hops[i], others[i - 1] = tick(hops[i], others[i - 1])
        others.append(swap(hops[i], "x"))
        if i < 3:
            cot_hops[i + 1], _ = tick(cot_hops[i + 1], hops[i])
            cot_others.append(swap(cot_hops[i + 1], "x"))
    gate_moved, up_moved, down_y, _ = tick(gate_moved, up_moved, down_y, hops[3])
    w_gate = jnp.where(y == z1, gu_sent[0], gate_moved)
    w_up = jnp.where(y == z1, up_sent, up_moved)
    down_half = jnp.concatenate([down_pair, down_y], axis=0)
    rows = w_down.shape[0]
    down = assemble(
        [(down_half[i * rows : (i + 1) * rows], (group ^ i) * rows, 0) for i in range(4)],
        (width, 2 * units),
    )
    ff_chunks = [with_partner(*item) for item in zip(hops, others)]
    cot_chunks = [with_partner(*item) for item in zip(cot_hops, cot_others)]

    hiddens, gate_grads, up_grads, back_parts, mlp_parts = [], [], [], [], []
    for rows_in, rows_cot in zip(ff_chunks, cot_chunks):
        gate, up = dot(rows_in, w_gate, 1, 1), dot(rows_in, w_up, 1, 1)
        sigmoid_gate = jax.nn.sigmoid(gate)
        silu = gate * sigmoid_gate
        hidden = (silu * up).astype(BF)
        grad_hidden = dot(rows_cot, down, 1, 0)
        grad_gate = (grad_hidden * up * sigmoid_gate * (1.0 + gate * (1.0 - sigmoid_gate))).astype(BF)
        grad_up = (grad_hidden * silu).astype(BF)
        back_parts.append(fold_core(dot(grad_gate, w_gate, 1, 0) + dot(grad_up, w_up, 1, 0)))
        mlp_parts.append(dot(hidden, down, 1, 1).astype(BF))
        hiddens.append(hidden)
        gate_grads.append(grad_gate)
        up_grads.append(grad_up)
    grad_normed_two = fold_hops([fold_plane(item, "x") for item in back_parts])

    ff_in, cot_all = jnp.concatenate(ff_chunks, axis=0), jnp.concatenate(cot_chunks, axis=0)
    gu_grad = jnp.stack(
        [dot(jnp.concatenate(parts, axis=0), ff_in, 0, 0).astype(BF) for parts in (gate_grads, up_grads)]
    )
    gu_own, gu_other = split(gu_grad, 1, y)
    down_grad = dot(cot_all, jnp.concatenate(hiddens, axis=0), 0, 0).astype(BF)
    down_own, down_other = split(down_grad, 1, y)
    gu_other, down_other = swap(gu_other, "y"), swap(down_other, "y")

    grad_normed_two, *mlp_parts = tick(grad_normed_two, *mlp_parts)
    mlp_parts = [fold_core(item) for item in mlp_parts]
    grad_norm_two, grad_gain_two = rms_back(grad_normed_two, residual, scale_two, gain_two)
    grad_residual = cotangent[0].astype(F32) + grad_norm_two
    grad_branch = grad_residual.astype(BF)
    grad_attended = dot(grad_branch, out_full, 1, 0).astype(BF)
    grad_slots = reorder(to_slots_kernel, place, grad_attended, (16, BLK, 128))
    grad_slots, *mlp_parts = tick(grad_slots, *mlp_parts)
    pieces = send_hops(grad_slots.reshape(4, 2, 2, BLK, 128))
    mlp_parts = [fold_plane(item, "x") for item in mlp_parts]
    pieces = send_core(send_plane(pieces, "y"))
    grad_branch, pieces, gu_other, down_other = tick(grad_branch, pieces, gu_other, down_other)
    branch_hops = [grad_branch] + [hop(grad_branch, j) for j in ORDER[1:]]
    branch_others = [swap(grad_branch, "y")]
    grad_proj = attend_back(place, saved, pieces, cosine, sine).reshape(16 * BLK, 384)
    back_parts = [fold_core(dot(grad_proj[j * quarter : (j + 1) * quarter], heads_qkv, 1, 0)) for j in range(4)]
    back_parts = tick(*back_parts, *mlp_parts, *branch_hops[1:], branch_others[0])
    mlp_parts, branch_hops[1:], branch_others = back_parts[4:8], back_parts[8:11], [back_parts[11]]
    back_parts = [fold_plane(item, "y") for item in back_parts[:4]]
    mlp_term = fold_hops(mlp_parts)
    layer_out = (residual + mlp_term).astype(BF)
    qkv_grad = dot(grad_proj, normed_all, 0, 0)
    gain_part = jnp.sum(qkv_grad * heads_qkv.astype(F32), axis=0) / gain_one
    qkv_own, qkv_other = split(qkv_grad.reshape(3, 2 * HD, width), 1, x)
    qkv_other = swap(qkv_other.astype(BF), "x")
    back_parts = tick(*back_parts, mlp_term, qkv_other)
    mlp_term, qkv_other, back_parts = back_parts[4], back_parts[5], back_parts[:4]
    grad_normed_one = fold_hops(back_parts)
    branch_others += [swap(item, "y") for item in branch_hops[1:]]
    grad_qkv = jnp.transpose(move(qkv_own + qkv_other.astype(F32), attn_place), (1, 0, 2))
    grad_gate_up = jnp.transpose(move(gu_own.astype(F32) + gu_other.astype(F32), ff_place), (1, 0, 2))
    grad_down = move(down_own.astype(F32) + down_other.astype(F32), ff_place)
    branch_all = jnp.concatenate([with_partner(*item) for item in zip(branch_hops, branch_others)], axis=0)
    out_grad = dot(branch_all, low_slots.reshape(16 * BLK, 128), 0, 0)
    out_own, out_other = split(out_grad, 1, x)
    grad_out_proj = move(out_own + swap(out_other.astype(BF), "x").astype(F32), attn_place)

    weighted = grad_normed_one * gain_one
    inner_mean = jnp.mean(weighted * inputs, axis=-1, keepdims=True)
    grad_input = grad_residual + scale_one * weighted - inputs * scale_one**3 * inner_mean

    gains = jnp.stack([gain_part, grad_gain_two])
    for name, bit in (("y", y), ("x", x)):
        mine, other = split(gains, 1, bit)
        gains = mine + swap(other, name)
    size = gains.shape[1] // 4
    quarters = [lax.dynamic_slice_in_dim(gains, (z ^ j) * size, size, 1) for j in range(4)]
    gains = quarters[0] + hop(quarters[1], 1) + hop(quarters[2], 2) + hop(quarters[3], 3)
    mine, other = split(gains, 1, c)
    gains = mine + swap(other, "c")
    return (
        layer_out[None],
        grad_input[None],
        gains[0],
        gains[1],
        grad_qkv,
        grad_out_proj,
        grad_gate_up,
        grad_down,
    )


def solution(mesh):
    if mesh.shape["fsdp"] != 4 or mesh.shape["seq"] != 8:
        return general_solution(mesh)
    fine = Mesh(mesh.devices.reshape(2, 2, 4, 2), AXES)
    fsdp, seq = ("y", "x"), ("z", "c")
    tokens = P(fsdp, seq, None)
    return jax.shard_map(
        body,
        mesh=fine,
        in_specs=(
            tokens,
            P(),
            P(),
            P(fsdp, None, None),
            P(fsdp, None),
            P(fsdp, None, None),
            P(fsdp, None),
            tokens,
        ),
        out_specs=(
            tokens,
            tokens,
            P(fsdp + seq),
            P(fsdp + seq),
            P(seq + fsdp, None, None),
            P(None, seq + fsdp),
            P(seq + fsdp, None, None),
            P(None, seq + fsdp),
        ),
        check_vma=False,
    )
```

```python
import functools
import math

import jax
import jax.numpy as jnp
from jax import lax
from jax.experimental import pallas as pl
from jax.experimental.pallas import tpu as pltpu
from jax.sharding import Mesh
from jax.sharding import PartitionSpec as P

HD = 64


NORM_EPS = 1e-05
ROPE_BASE = 130000.0


def rotate(matrix):
    shaped = matrix.reshape(matrix.shape[:-1] + (matrix.shape[-1] // HD, 2, HD // 2))
    turned = jnp.stack([-shaped[..., 1, :], shaped[..., 0, :]], axis=-2)
    return turned.reshape(matrix.shape)


def rotate_back(matrix):
    shaped = matrix.reshape(matrix.shape[:-1] + (matrix.shape[-1] // HD, 2, HD // 2))
    turned = jnp.stack([shaped[..., 1, :], -shaped[..., 0, :]], axis=-2)
    return turned.reshape(matrix.shape)


def rope_tables(positions, columns):
    freq_index = (jnp.arange(columns, dtype=jnp.int32) % (HD // 2)).astype(jnp.float32)
    inverse = ROPE_BASE ** (-2.0 * freq_index / HD)
    angles = positions.astype(jnp.float32)[:, None] * inverse[None, :]
    return (jnp.cos(angles), jnp.sin(angles))


def rms_scale(matrix):
    return lax.rsqrt(jnp.mean(matrix * matrix, axis=-1, keepdims=True) + NORM_EPS)


def rms_back(grad_normed, matrix, scale_rows, gain):
    weighted = grad_normed * gain
    inner_mean = jnp.mean(weighted * matrix, axis=-1, keepdims=True)
    grad_matrix = scale_rows * weighted - matrix * scale_rows**3 * inner_mean
    grad_gain = jnp.sum(grad_normed * matrix * scale_rows, axis=0)
    return (grad_matrix, grad_gain)


def attend_forward(queries, key_rows, values):
    seq_count, length, width_here = queries.shape
    heads_here = width_here // HD
    q_block = min(512, length)
    k_block = min(256, length)
    inv_root = 1.0 / math.sqrt(HD)
    shaped_q = queries.reshape(seq_count, length, heads_here, HD)
    shaped_k = key_rows.reshape(seq_count, length, heads_here, HD)
    shaped_v = values.reshape(seq_count, length, heads_here, HD)

    def query_step(q_index, carried):
        attended, totals = carried
        offset = q_index * q_block
        q_rows = lax.dynamic_slice_in_dim(shaped_q, offset, q_block, 1)
        query_pos = offset + jnp.arange(q_block, dtype=jnp.int32)

        def key_step(k_index, running):
            unnorm, denominator = running
            k_start = k_index * k_block
            k_rows = lax.dynamic_slice_in_dim(shaped_k, k_start, k_block, 1)
            v_rows = lax.dynamic_slice_in_dim(shaped_v, k_start, k_block, 1)
            scores = (
                jnp.einsum("bqhd,bkhd->bhqk", q_rows, k_rows, preferred_element_type=jnp.float32)
                * inv_root
            )
            causal = (k_start + jnp.arange(k_block, dtype=jnp.int32))[None, :] <= query_pos[:, None]
            exp_scores = jnp.where(causal, jnp.exp(scores), 0.0)
            denominator = denominator + jnp.sum(exp_scores, axis=-1)
            unnorm = unnorm + jnp.einsum(
                "bhqk,bkhd->bqhd",
                exp_scores.astype(jnp.bfloat16),
                v_rows,
                preferred_element_type=jnp.float32,
            )
            return (unnorm, denominator)

        start_state = (
            jnp.zeros((seq_count, q_block, heads_here, HD), jnp.float32),
            jnp.zeros((seq_count, heads_here, q_block), jnp.float32),
        )
        unnorm, denominator = lax.fori_loop(0, (offset + q_block) // k_block, key_step, start_state)
        block_out = unnorm / jnp.transpose(denominator, (0, 2, 1))[..., None]
        attended = lax.dynamic_update_slice_in_dim(attended, block_out, offset, 1)
        totals = lax.dynamic_update_slice_in_dim(totals, denominator, offset, 2)
        return (attended, totals)

    initial = (
        jnp.zeros((seq_count, length, heads_here, HD), jnp.float32),
        jnp.zeros((seq_count, heads_here, length), jnp.float32),
    )
    attended, totals = lax.fori_loop(0, length // q_block, query_step, initial)
    return (attended.reshape(seq_count, length, width_here), totals)


def attend_backward(queries, key_rows, values, attended, totals, grad_attended):
    seq_count, length, width_here = queries.shape
    heads_here = width_here // HD
    q_block = min(512, length)
    k_block = min(256, length)
    inv_root = 1.0 / math.sqrt(HD)
    shaped_q = queries.reshape(seq_count, length, heads_here, HD)
    shaped_k = key_rows.reshape(seq_count, length, heads_here, HD)
    shaped_v = values.reshape(seq_count, length, heads_here, HD)
    shaped_grad = grad_attended.reshape(seq_count, length, heads_here, HD).astype(jnp.float32)
    shaped_att = attended.reshape(seq_count, length, heads_here, HD)
    totals_rows = jnp.transpose(totals, (0, 2, 1))
    grad_total = -jnp.sum(shaped_grad * shaped_att, axis=-1) / totals_rows
    grad_unnorm = (shaped_grad / totals_rows[..., None]).astype(jnp.bfloat16)

    def query_step(q_index, carried):
        grad_q, grad_k, grad_v = carried
        offset = q_index * q_block
        q_rows = lax.dynamic_slice_in_dim(shaped_q, offset, q_block, 1)
        g_rows = lax.dynamic_slice_in_dim(grad_unnorm, offset, q_block, 1)
        total_rows = jnp.transpose(
            lax.dynamic_slice_in_dim(grad_total, offset, q_block, 1), (0, 2, 1)
        )
        query_pos = offset + jnp.arange(q_block, dtype=jnp.int32)

        def key_step(k_index, running):
            dq_acc, dk_all, dv_all = running
            k_start = k_index * k_block
            k_rows = lax.dynamic_slice_in_dim(shaped_k, k_start, k_block, 1)
            v_rows = lax.dynamic_slice_in_dim(shaped_v, k_start, k_block, 1)
            scores = (
                jnp.einsum("bqhd,bkhd->bhqk", q_rows, k_rows, preferred_element_type=jnp.float32)
                * inv_root
            )
            causal = (k_start + jnp.arange(k_block, dtype=jnp.int32))[None, :] <= query_pos[:, None]
            exp_scores = jnp.where(causal, jnp.exp(scores), 0.0)
            grad_prob = jnp.einsum(
                "bqhd,bkhd->bhqk", g_rows, v_rows, preferred_element_type=jnp.float32
            )
            grad_scores = (exp_scores * (grad_prob + total_rows[..., None])).astype(jnp.bfloat16)
            dq_acc = (
                dq_acc
                + jnp.einsum(
                    "bhqk,bkhd->bqhd", grad_scores, k_rows, preferred_element_type=jnp.float32
                )
                * inv_root
            )
            dk_part = (
                jnp.einsum(
                    "bhqk,bqhd->bkhd", grad_scores, q_rows, preferred_element_type=jnp.float32
                )
                * inv_root
            )
            dv_part = jnp.einsum(
                "bhqk,bqhd->bkhd",
                exp_scores.astype(jnp.bfloat16),
                g_rows,
                preferred_element_type=jnp.float32,
            )
            dk_slice = lax.dynamic_slice_in_dim(dk_all, k_start, k_block, 1) + dk_part
            dv_slice = lax.dynamic_slice_in_dim(dv_all, k_start, k_block, 1) + dv_part
            dk_all = lax.dynamic_update_slice_in_dim(dk_all, dk_slice, k_start, 1)
            dv_all = lax.dynamic_update_slice_in_dim(dv_all, dv_slice, k_start, 1)
            return (dq_acc, dk_all, dv_all)

        start_state = (jnp.zeros((seq_count, q_block, heads_here, HD), jnp.float32), grad_k, grad_v)
        dq_block, grad_k, grad_v = lax.fori_loop(
            0, (offset + q_block) // k_block, key_step, start_state
        )
        grad_q = lax.dynamic_update_slice_in_dim(grad_q, dq_block, offset, 1)
        return (grad_q, grad_k, grad_v)

    empty = jnp.zeros((seq_count, length, heads_here, HD), jnp.float32)
    grad_q, grad_k, grad_v = lax.fori_loop(0, length // q_block, query_step, (empty, empty, empty))
    cosine, sine_table = rope_tables(jnp.arange(length, dtype=jnp.int32), width_here)
    grad_q = grad_q.reshape(seq_count, length, width_here)
    grad_k = grad_k.reshape(seq_count, length, width_here)
    grad_v = grad_v.reshape(seq_count, length, width_here)
    raw_q = grad_q * cosine + rotate_back(grad_q * sine_table)
    raw_k = grad_k * cosine + rotate_back(grad_k * sine_table)
    return jnp.stack([raw_q, raw_k, grad_v]).astype(jnp.bfloat16)


def general_body(residual_in, attn_gain, mlp_gain, w_qkv, w_out, w_gate_up, w_down, cotangent):
    seq_count, shard_len, model_width = residual_in.shape
    tokens = seq_count * shard_len
    seq_index = lax.axis_index("seq")
    positions = seq_index * shard_len + jnp.arange(tokens, dtype=jnp.int32) % shard_len
    cosine, sine_table = rope_tables(positions, model_width)
    inputs = residual_in.reshape(tokens, model_width).astype(jnp.float32)
    gain_one = attn_gain.astype(jnp.float32)
    gain_two = mlp_gain.astype(jnp.float32)
    scale_one = rms_scale(inputs)
    normed_one = (inputs * scale_one * gain_one).astype(jnp.bfloat16)
    qkv_full, out_full = (
        lax.all_gather(w_qkv, "fsdp", axis=0, tiled=True),
        lax.all_gather(w_out, "fsdp", axis=0, tiled=True),
    )
    projected = jnp.einsum("td,fpd->ptf", normed_one, qkv_full, preferred_element_type=jnp.float32)
    queries = (projected[0] * cosine + rotate(projected[0]) * sine_table).astype(jnp.bfloat16)
    key_rows = (projected[1] * cosine + rotate(projected[1]) * sine_table).astype(jnp.bfloat16)
    values = projected[2].astype(jnp.bfloat16)
    stacked = jnp.stack([queries, key_rows, values]).reshape(3, seq_count, shard_len, model_width)
    head_view = lax.all_to_all(stacked, "seq", split_axis=3, concat_axis=2, tiled=True)
    attended, totals = attend_forward(head_view[0], head_view[1], head_view[2])
    attended_heads = attended.astype(jnp.bfloat16)
    sent_back = lax.all_to_all(attended_heads, "seq", split_axis=1, concat_axis=2, tiled=True)
    attended_low = sent_back.reshape(tokens, model_width)
    branch = jnp.einsum("ti,fi->tf", attended_low, out_full, preferred_element_type=jnp.float32)
    residual = inputs + branch
    scale_two = rms_scale(residual)
    normed_two = (residual * scale_two * gain_two).astype(jnp.bfloat16)
    up_full, down_full = (
        lax.all_gather(w_gate_up, "fsdp", axis=0, tiled=True),
        lax.all_gather(w_down, "fsdp", axis=0, tiled=True),
    )
    gate_up = jnp.einsum("td,jpd->ptj", normed_two, up_full, preferred_element_type=jnp.float32)
    hidden = (jax.nn.silu(gate_up[0]) * gate_up[1]).astype(jnp.bfloat16)
    mlp_term = jnp.einsum("tj,fj->tf", hidden, down_full, preferred_element_type=jnp.float32)
    layer_out = (
        (residual + mlp_term).astype(jnp.bfloat16).reshape(seq_count, shard_len, model_width)
    )
    grad_out = cotangent.reshape(tokens, model_width)
    up_again, down_again = (
        lax.all_gather(w_gate_up, "fsdp", axis=0, tiled=True),
        lax.all_gather(w_down, "fsdp", axis=0, tiled=True),
    )
    grad_hidden = jnp.einsum("tf,fj->tj", grad_out, down_again, preferred_element_type=jnp.float32)
    sigmoid_gate = jax.nn.sigmoid(gate_up[0])
    grad_gate = grad_hidden * gate_up[1] * sigmoid_gate * (1.0 + gate_up[0] * (1.0 - sigmoid_gate))
    grad_up = grad_hidden * jax.nn.silu(gate_up[0])
    grad_gu = jnp.stack([grad_gate, grad_up]).astype(jnp.bfloat16)
    grad_normed_two = jnp.einsum(
        "ptj,jpd->td", grad_gu, up_again, preferred_element_type=jnp.float32
    )
    ff_width = grad_gu.shape[2]
    unit_rows = jnp.concatenate([grad_gu, hidden[None]], axis=0).reshape(
        3, seq_count, shard_len, ff_width
    )
    unit_cols = lax.all_to_all(unit_rows, "seq", split_axis=3, concat_axis=2, tiled=True)
    normed_piece = lax.all_gather(
        normed_two.reshape(seq_count, shard_len, model_width), "seq", axis=1, tiled=True
    )
    grad_piece = lax.all_gather(cotangent, "seq", axis=1, tiled=True)
    gu_part = jnp.einsum(
        "psnj,snd->jpd", unit_cols[:2], normed_piece, preferred_element_type=jnp.float32
    )
    down_part = jnp.einsum(
        "snf,snj->fj", grad_piece, unit_cols[2], preferred_element_type=jnp.float32
    )
    gu_part, down_part = (gu_part, down_part)
    grad_gate_up, grad_down = (
        lax.psum_scatter(
            gu_part.astype(jnp.bfloat16), "fsdp", scatter_dimension=0, tiled=True
        ).astype(jnp.float32),
        lax.psum_scatter(
            down_part.astype(jnp.bfloat16), "fsdp", scatter_dimension=1, tiled=True
        ).astype(jnp.float32),
    )
    grad_norm_two, grad_gain_two = rms_back(grad_normed_two, residual, scale_two, gain_two)
    grad_residual = grad_out.astype(jnp.float32) + grad_norm_two
    qkv_back, out_back = (
        lax.all_gather(w_qkv, "fsdp", axis=0, tiled=True),
        lax.all_gather(w_out, "fsdp", axis=0, tiled=True),
    )
    grad_branch = grad_residual.astype(jnp.bfloat16)
    grad_attended = jnp.einsum(
        "tf,fi->ti", grad_branch, out_back, preferred_element_type=jnp.float32
    )
    grad_attended = grad_attended.astype(jnp.bfloat16).reshape(seq_count, shard_len, model_width)
    grad_heads = lax.all_to_all(grad_attended, "seq", split_axis=2, concat_axis=1, tiled=True)
    grad_stacked = attend_backward(
        head_view[0], head_view[1], head_view[2], attended, totals, grad_heads
    )
    normed_piece = lax.all_gather(
        normed_one.reshape(seq_count, shard_len, model_width), "seq", axis=1, tiled=True
    )
    branch_piece = lax.all_gather(
        grad_branch.reshape(seq_count, shard_len, model_width), "seq", axis=1, tiled=True
    )
    grad_piece = grad_stacked
    qkv_part = jnp.einsum(
        "psnf,snd->fpd", grad_piece, normed_piece, preferred_element_type=jnp.float32
    )
    out_part = jnp.einsum(
        "snf,sni->fi", branch_piece, attended_heads, preferred_element_type=jnp.float32
    )
    qkv_part, out_part = (qkv_part, out_part)
    grad_qkv, grad_out_proj = (
        lax.psum_scatter(
            qkv_part.astype(jnp.bfloat16), "fsdp", scatter_dimension=0, tiled=True
        ).astype(jnp.float32),
        lax.psum_scatter(
            out_part.astype(jnp.bfloat16), "fsdp", scatter_dimension=1, tiled=True
        ).astype(jnp.float32),
    )
    grad_projected = lax.all_to_all(grad_stacked, "seq", split_axis=2, concat_axis=3, tiled=True)
    grad_projected = grad_projected.reshape(3, tokens, model_width)
    grad_normed_one = jnp.einsum(
        "ptf,fpd->td", grad_projected, qkv_back, preferred_element_type=jnp.float32
    )
    grad_norm_one, grad_gain_one = rms_back(grad_normed_one, inputs, scale_one, gain_one)
    grad_input = (grad_residual + grad_norm_one).reshape(seq_count, shard_len, model_width)
    grad_attn_gain, grad_mlp_gain = (
        lax.psum_scatter(grad_gain_one, ("fsdp", "seq"), scatter_dimension=0, tiled=True),
        lax.psum_scatter(grad_gain_two, ("fsdp", "seq"), scatter_dimension=0, tiled=True),
    )
    return (
        layer_out,
        grad_input,
        grad_attn_gain,
        grad_mlp_gain,
        grad_qkv,
        grad_out_proj,
        grad_gate_up,
        grad_down,
    )


def general_solution(mesh):
    return jax.shard_map(
        general_body,
        mesh=mesh,
        in_specs=(
            P("fsdp", "seq", None),
            P(),
            P(),
            P("fsdp", None, None),
            P("fsdp", None),
            P("fsdp", None, None),
            P("fsdp", None),
            P("fsdp", "seq", None),
        ),
        out_specs=(
            P("fsdp", "seq", None),
            P("fsdp", "seq", None),
            P(("fsdp", "seq")),
            P(("fsdp", "seq")),
            P(("seq", "fsdp"), None, None),
            P(None, ("seq", "fsdp")),
            P(("seq", "fsdp"), None, None),
            P(None, ("seq", "fsdp")),
        ),
        check_vma=False,
    )


BF = jnp.bfloat16
F32 = jnp.float32
AXES = ("y", "x", "z", "c")
PAIR = [(0, 1), (1, 0)]
BLK = 128
ORDER = (0, 1, 3, 2)
Q_ROWS = 256


def swap(value, axis):
    return lax.ppermute(value, axis, PAIR)


def hop(value, dist):
    return lax.ppermute(value, "z", [(i, i ^ dist) for i in range(4)])


def tick(*values):
    return lax.optimization_barrier(values)


def with_partner(held, other):
    both = jnp.concatenate([held, other], axis=0)
    return jnp.concatenate([both, swap(both, "c")], axis=0)


def fold_core(part):
    n = part.shape[0] // 2
    return part[:n].astype(F32) + swap(part[n:].astype(BF), "c").astype(F32)


def fold_plane(kept, plane):
    n = kept.shape[0] // 2
    return kept[:n] + swap(kept[n:].astype(BF), plane).astype(F32)


def fold_hops(parts):
    total = parts[0]
    for j, part in zip(ORDER[1:], parts[1:]):
        total = total + hop(part.astype(BF), j).astype(F32)
    return total


def send_core(pieces):
    return jnp.stack([pieces[:, 0], swap(pieces[:, 1], "c")], axis=1)


def send_plane(pieces, plane):
    return jnp.stack([pieces[:, :, 0], swap(pieces[:, :, 1], plane)], axis=2)


def send_hops(pieces):
    return jnp.stack([hop(pieces[i], j) if j else pieces[i] for i, j in enumerate(ORDER)])


def turn(value, back):
    lane = lax.broadcasted_iota(jnp.int32, value.shape, 1) % HD
    up = pltpu.roll(value, HD // 2, 1)
    down = pltpu.roll(value, value.shape[1] - HD // 2, 1)
    return jnp.where(lane < HD // 2, down, -up) if back else jnp.where(lane < HD // 2, -down, up)


def head_mask(value, head):
    lane = lax.broadcasted_iota(jnp.int32, value.shape, 1)
    return jnp.where((lane < HD) == (head == 0), value, jnp.zeros_like(value))


def dot(left, right, left_dim, right_dim):
    return lax.dot_general(
        left, right, (((left_dim,), (right_dim,)), ((), ())), preferred_element_type=F32
    )


def causal_exp(scores, start):
    rows, cols = scores.shape
    query = start + lax.broadcasted_iota(jnp.int32, (rows, rows), 0)
    key = cols - rows + lax.broadcasted_iota(jnp.int32, (rows, rows), 1)
    last = jnp.where(key <= query, jnp.exp(scores[:, cols - rows :]), 0.0)
    if cols == rows:
        return last
    return jnp.concatenate([jnp.exp(scores[:, : cols - rows]), last], axis=1)


def chunk_of(slot):
    dist = slot >> 1
    return dist ^ (dist >> 1)


def attend_kernel(place, proj, cosine, sine, q_out, k_out, v_out, att_out, den_out, low_out):
    length = q_out.shape[1]
    me = place[0]
    for block in range(length // BLK):
        slot = me ^ block
        here = proj[chunk_of(slot), slot & 1, 0]
        rows = slice(block * BLK, (block + 1) * BLK)
        cos_rows, sin_rows = cosine[rows, :], sine[rows, :]
        raw_q, raw_k = here[:, :128], here[:, 128:256]
        q_out[0, rows, :] = (raw_q * cos_rows + turn(raw_q, False) * sin_rows).astype(BF)
        k_out[0, rows, :] = (raw_k * cos_rows + turn(raw_k, False) * sin_rows).astype(BF)
        v_out[0, rows, :] = here[:, 256:].astype(BF)
    for start in range(0, length, Q_ROWS):
        seen = start + Q_ROWS
        queries = q_out[0, start:seen, :] * jnp.asarray(0.125, BF)
        keys, values = k_out[0, :seen, :], v_out[0, :seen, :]
        unnorm, den = None, None
        for head in range(2):
            exp_scores = causal_exp(dot(head_mask(queries, head), keys, 1, 1), start)
            total = jnp.sum(exp_scores, axis=1, keepdims=True)
            part = dot(exp_scores.astype(BF), head_mask(values, head), 1, 0)
            total = head_mask(jnp.broadcast_to(total, part.shape), head)
            unnorm = part if unnorm is None else unnorm + part
            den = total if den is None else den + total
        attended = unnorm / den
        att_out[0, start:seen, :] = attended
        den_out[0, start:seen, :] = den
        for block in range(start // BLK, seen // BLK):
            slot = me ^ block
            first = block * BLK - start
            low_out[chunk_of(slot), slot & 1, 0] = attended[first : first + BLK].astype(BF)


def attend_back_kernel(
    place, q_ref, k_ref, v_ref, att_ref, den_ref, grad_ref, cosine, sine, out, grad, grad_q, grad_k, grad_v
):
    length = q_ref.shape[1]
    me = place[0]
    for block in range(length // BLK):
        slot = me ^ block
        grad[block * BLK : (block + 1) * BLK, :] = grad_ref[chunk_of(slot), slot & 1, 0].astype(F32)
    grad_k[...] = jnp.zeros_like(grad_k)
    grad_v[...] = jnp.zeros_like(grad_v)
    for start in range(0, length, Q_ROWS):
        seen = start + Q_ROWS
        queries = q_ref[0, start:seen, :] * jnp.asarray(0.125, BF)
        keys, values = k_ref[0, :seen, :], v_ref[0, :seen, :]
        grad_rows, den = grad[start:seen, :], den_ref[0, start:seen, :]
        unnorm = (grad_rows / den).astype(BF)
        weighted = grad_rows * att_ref[0, start:seen, :] / den
        total_q = None
        for head in range(2):
            q_head, g_head = head_mask(queries, head), head_mask(unnorm, head)
            exp_scores = causal_exp(dot(q_head, keys, 1, 1), start)
            grad_total = -jnp.sum(head_mask(weighted, head), axis=1, keepdims=True)
            grad_scores = (exp_scores * (dot(g_head, values, 1, 1) + grad_total)).astype(BF)
            part = dot(grad_scores, head_mask(keys, head), 1, 0)
            total_q = part if total_q is None else total_q + part
            grad_k[:seen, :] += dot(grad_scores, q_head, 0, 0)
            grad_v[:seen, :] += dot(exp_scores.astype(BF), g_head, 0, 0)
        grad_q[start:seen, :] = total_q * 0.125
    for block in range(length // BLK):
        slot = me ^ block
        rows = slice(block * BLK, (block + 1) * BLK)
        cos_rows, sin_rows = cosine[rows, :], sine[rows, :]
        for part, held in enumerate((grad_q, grad_k)):
            value = held[rows, :]
            raw = value * cos_rows + turn(value * sin_rows, True)
            out[chunk_of(slot), slot & 1, 0, :, part * 128 : (part + 1) * 128] = raw.astype(BF)
        out[chunk_of(slot), slot & 1, 0, :, 256:] = grad_v[rows, :].astype(BF)


def whole(shape):
    return pl.BlockSpec(shape, lambda i, place: (0,) * len(shape))


def per_seq(shape, at):
    return pl.BlockSpec(shape, lambda i, place: tuple(i if d == at else 0 for d in range(len(shape))))


def attend(place, proj, cosine, sine):
    length = cosine.shape[0]
    seq = jax.ShapeDtypeStruct((2, length, 128), BF)
    wide = jax.ShapeDtypeStruct((2, length, 128), F32)
    return pl.pallas_call(
        attend_kernel,
        grid_spec=pltpu.PrefetchScalarGridSpec(
            num_scalar_prefetch=1,
            grid=(2,),
            in_specs=[per_seq((4, 2, 1, BLK, 384), 2), whole((length, 128)), whole((length, 128))],
            out_specs=[per_seq((1, length, 128), 0)] * 5 + [per_seq((4, 2, 1, BLK, 128), 2)],
        ),
        out_shape=[seq, seq, seq, wide, wide, jax.ShapeDtypeStruct((4, 2, 2, BLK, 128), BF)],
        compiler_params=pltpu.CompilerParams(vmem_limit_bytes=40 << 20),
        cost_estimate=pl.CostEstimate(flops=0, bytes_accessed=1 << 20, transcendentals=0),
        name="attend",
    )(place, proj, cosine, sine)


def attend_back(place, saved, grad_slots, cosine, sine):
    length = cosine.shape[0]
    return pl.pallas_call(
        attend_back_kernel,
        grid_spec=pltpu.PrefetchScalarGridSpec(
            num_scalar_prefetch=1,
            grid=(2,),
            in_specs=[per_seq((1, length, 128), 0)] * 5
            + [per_seq((4, 2, 1, BLK, 128), 2), whole((length, 128)), whole((length, 128))],
            out_specs=per_seq((4, 2, 1, BLK, 384), 2),
            scratch_shapes=[pltpu.VMEM((length, 128), F32)] * 4,
        ),
        out_shape=jax.ShapeDtypeStruct((4, 2, 2, BLK, 384), BF),
        compiler_params=pltpu.CompilerParams(vmem_limit_bytes=40 << 20),
        cost_estimate=pl.CostEstimate(flops=0, bytes_accessed=1 << 20, transcendentals=0),
        name="attend_back",
    )(place, *saved, grad_slots, cosine, sine)


def perm_of(target):
    pairs = []
    for index in range(32):
        bits = [(index >> shift) & 1 for shift in (4, 3, 2, 1, 0)]
        place = 0
        for bit in target(*bits):
            place = 2 * place + bit
        pairs.append((index, place))
    return pairs


def join_kernel(place, half, other, out):
    cols = half.shape[1]

    @pl.when(place[3] == 0)
    def _():
        out[:, :cols] = half[...]
        out[:, cols:] = other[...]

    @pl.when(place[3] != 0)
    def _():
        out[:, :cols] = other[...]
        out[:, cols:] = half[...]


def join_out(place, half, other):
    rows, cols = half.shape[0] // 4, half.shape[1]
    block = pl.BlockSpec((rows, cols), lambda i, place: (i, 0))
    return pl.pallas_call(
        join_kernel,
        grid_spec=pltpu.PrefetchScalarGridSpec(
            num_scalar_prefetch=1,
            grid=(4,),
            in_specs=[block, block],
            out_specs=pl.BlockSpec(
                (rows, 2 * cols), lambda i, place: (place[2] ^ (((i & 1) << 1) | (i >> 1)), 0)
            ),
        ),
        out_shape=jax.ShapeDtypeStruct((4 * rows, 2 * cols), BF),
        cost_estimate=pl.CostEstimate(flops=0, bytes_accessed=1 << 20, transcendentals=0),
        name="join_out",
    )(place, half, other)


def order_kernel(place, block, out):
    out[...] = block[...]


def order_rows(place, value):
    rows, cols = value.shape[0] // 4, value.shape[1]
    return pl.pallas_call(
        order_kernel,
        grid_spec=pltpu.PrefetchScalarGridSpec(
            num_scalar_prefetch=1,
            grid=(4,),
            in_specs=[pl.BlockSpec((rows, cols), lambda i, place: (i, 0))],
            out_specs=pl.BlockSpec((rows, cols), lambda i, place: (place[2] ^ i, 0)),
        ),
        out_shape=jax.ShapeDtypeStruct(value.shape, BF),
        cost_estimate=pl.CostEstimate(flops=0, bytes_accessed=1 << 20, transcendentals=0),
        name="order_rows",
    )(place, value)


def slot_of(rel):
    bit_y, bit_z0, bit_c, bit_z1 = rel >> 3, (rel >> 2) & 1, (rel >> 1) & 1, rel & 1
    return ORDER.index(2 * bit_z1 + bit_z0) * 4 + bit_c * 2 + bit_y


def to_heads_kernel(place, slots, out):
    for rel in range(16):
        pair = place[1] ^ rel
        out[:, pl.ds(pl.multiple_of(pair * 128, 128), 128)] = slots[slot_of(rel)]


def to_slots_kernel(place, rows, out):
    for rel in range(16):
        pair = place[1] ^ rel
        out[slot_of(rel)] = rows[:, pl.ds(pl.multiple_of(pair * 128, 128), 128)]


def reorder(kernel, place, value, shape):
    return pl.pallas_call(
        kernel,
        in_specs=[pl.BlockSpec(memory_space=pltpu.SMEM), pl.BlockSpec(memory_space=pltpu.VMEM)],
        out_specs=pl.BlockSpec(memory_space=pltpu.VMEM),
        out_shape=jax.ShapeDtypeStruct(shape, BF),
        cost_estimate=pl.CostEstimate(flops=0, bytes_accessed=1 << 20, transcendentals=0),
        name=kernel.__name__,
    )(place, value)


def split(value, dim, bit):
    size = value.shape[dim] // 2
    return (
        lax.dynamic_slice_in_dim(value, bit * size, size, dim),
        lax.dynamic_slice_in_dim(value, (1 - bit) * size, size, dim),
    )


def ff_place(at_y, at_x, at_z1, at_z0, at_c):
    return at_y, at_z0, at_z1, at_x, at_c


def attn_place(at_y, at_x, at_z1, at_z0, at_c):
    return at_z1, at_x, at_y, at_z0, at_c


def move(value, target):
    return lax.ppermute(value.astype(BF), AXES, perm_of(target)).astype(F32)


def body(residual_in, attn_gain, mlp_gain, w_qkv, w_out, w_gate_up, w_down, cotangent):
    y, x, z, c = [lax.axis_index(name) for name in AXES]
    z1, z0 = z >> 1, z & 1
    group, part = 2 * y + x, 2 * z + c
    width = residual_in.shape[2]
    length = BLK * 8
    quarter = 4 * BLK
    units = w_gate_up.shape[0] // 8
    inputs = residual_in[0].astype(F32)
    gain_one, gain_two = attn_gain.astype(F32), mlp_gain.astype(F32)
    scale_one = rms_scale(inputs)
    normed_one = (inputs * scale_one * gain_one).astype(BF)

    qkv_sent = lax.dynamic_slice_in_dim(w_qkv, (4 * c + 2 * z1) * HD, 2 * HD, 0)
    qkv_sent = jnp.transpose(qkv_sent, (1, 0, 2)).reshape(3 * 2 * HD, width)
    x_pairs = [((i & 1) * 4 + i, (1 - (i & 1)) * 4 + i) for i in range(4)]
    y_pairs = [((i >> 1) * 4 + i, (1 - (i >> 1)) * 4 + i) for i in range(4)]
    hops = [normed_one] + [hop(normed_one, j) for j in ORDER[1:]]
    others = [swap(normed_one, "y")]
    qkv_moved = lax.ppermute(qkv_sent, ("x", "z"), x_pairs)
    cols = width // 2
    out_own = lax.dynamic_slice_in_dim(w_out, c * cols, cols, 1)
    hops[3], qkv_moved = tick(hops[3], qkv_moved)
    others += [swap(held, "y") for held in hops[1:]]
    normed_all = jnp.concatenate([with_partner(*item) for item in zip(hops, others)], axis=0)
    heads_qkv = jnp.where(x == z0, qkv_sent, qkv_moved)

    def columns(side):
        first = (8 * (2 * z1 + side) + 4 * c + z0) * units
        return jnp.concatenate(
            [lax.dynamic_slice_in_dim(w_down, first + 2 * j * units, units, 1) for j in range(2)], axis=1
        )

    gu_sent = [lax.dynamic_slice_in_dim(w_gate_up, (4 * c + 2 * j + z0) * units, units, 0) for j in range(2)]
    gate_sent = [jnp.reshape(item[:, 0], (units, width)) for item in gu_sent]
    up_sent = [jnp.reshape(item[:, 1], (units, width)) for item in gu_sent]
    down_own, down_sent = columns(x), columns(1 - x)

    def to_y(value):
        return lax.ppermute(value, ("y", "z"), y_pairs)

    cos_half, sin_half = rope_tables(jnp.arange(length, dtype=jnp.int32), HD // 2)
    cosine, sine = jnp.tile(cos_half, (1, 4)), jnp.tile(sin_half, (1, 4))
    place = jnp.stack([part, 8 * y + 4 * z0 + 2 * c + z1, group, c]).astype(jnp.int32)

    *firsts, cot, out_own, down_sent, down_own = tick(
        normed_all, heads_qkv, *gate_sent, *up_sent, cosine, sine, place, cotangent[0], out_own, down_sent, down_own
    )
    normed_all, heads_qkv, gate_sent, up_sent = firsts[0], firsts[1], firsts[2:4], firsts[4:6]
    cosine, sine, place = firsts[6:]
    cot_hops = [cot, hop(cot, 1), hop(cot, 3), None]
    cot_others = [swap(cot, "x")]
    down_x = swap(down_sent, "x")
    out_y = swap(out_own, "y")

    proj = dot(normed_all, heads_qkv, 1, 1)
    *saved, low_slots = attend(place, proj.reshape(4, 2, 2, BLK, 384), cosine, sine)
    pieces = send_core(low_slots)
    pieces, out_y, cot_hops[1], cot_others[0], down_x = tick(pieces, out_y, cot_hops[1], cot_others[0], down_x)
    out_pair = jnp.concatenate([out_own, out_y], axis=0)
    out_x = swap(out_pair, "x")
    down_pair = jnp.concatenate([down_own, down_x], axis=0)
    down_y = swap(down_pair, "y")
    pieces = send_plane(pieces, "y")
    pieces, cot_hops[2] = tick(pieces, cot_hops[2])
    pieces = send_hops(pieces)
    pieces, out_x, down_y, gate_sent[0], cot = tick(pieces, out_x, down_y, gate_sent[0], cot)
    cot_hops[3] = hop(cot, 2)
    gate_moved = [to_y(gate_sent[0])]
    out_half = jnp.concatenate([out_pair, out_x], axis=0)
    out_c = swap(out_half, "c")
    attended = reorder(to_heads_kernel, place, pieces.reshape(16, BLK, 128), (BLK, width))
    out_full = join_out(place, out_half, out_c)
    attended, out_full, cot_hops[1], cot_hops[2] = tick(attended, out_full, cot_hops[1], cot_hops[2])
    cot_others += [swap(item, "x") for item in cot_hops[1:3]]
    residual = inputs + dot(attended, out_full, 1, 1)
    scale_two = rms_scale(residual)
    normed_two = (residual * scale_two * gain_two).astype(BF)

    normed_two, cot_hops[3], gate_moved[0], gate_sent[1] = tick(normed_two, cot_hops[3], gate_moved[0], gate_sent[1])
    gate_moved.append(to_y(gate_sent[1]))
    hops = [normed_two] + [hop(normed_two, j) for j in ORDER[1:]]
    others = [swap(normed_two, "x")]
    hops[1], gate_moved[1], up_sent[0], cot_others[1] = tick(hops[1], gate_moved[1], up_sent[0], cot_others[1])
    up_moved = [to_y(up_sent[0])]
    others.append(swap(hops[1], "x"))
    hops[2], up_moved[0], up_sent[1], cot_others[2], cot_hops[3] = tick(
        hops[2], up_moved[0], up_sent[1], cot_others[2], cot_hops[3]
    )
    up_moved.append(to_y(up_sent[1]))
    others.append(swap(hops[2], "x"))
    cot_others.append(swap(cot_hops[3], "x"))
    others.append(swap(hops[3], "x"))
    w_gate, w_up = [
        jnp.concatenate([jnp.where(y == z1, own, moved) for own, moved in zip(held, arrived)], axis=0)
        for held, arrived in ((gate_sent, gate_moved), (up_sent, up_moved))
    ]
    down = order_rows(place, jnp.concatenate([down_pair, down_y], axis=0))
    ff_chunks = [with_partner(*item) for item in zip(hops, others)]
    cot_chunks = [with_partner(*item) for item in zip(cot_hops, cot_others)]

    hiddens, gate_grads, up_grads, back_parts, mlp_parts = [[None] * 4 for _ in range(5)]
    first, second, third, last = turns = (2, 3, 1, 0)
    for i in turns:
        if i == third:
            ff_chunks[i], back_parts[first] = tick(ff_chunks[i], back_parts[first])
            back_parts[first] = fold_plane(back_parts[first], "x")
        if i == last:
            ff_chunks[i], back_parts[second], back_parts[first] = tick(
                ff_chunks[i], back_parts[second], back_parts[first]
            )
            back_parts[second] = fold_plane(back_parts[second], "x")
        gate, up = dot(ff_chunks[i], w_gate, 1, 1), dot(ff_chunks[i], w_up, 1, 1)
        sigmoid_gate = jax.nn.sigmoid(gate)
        silu = gate * sigmoid_gate
        hidden = (silu * up).astype(BF)
        grad_hidden = dot(cot_chunks[i], down, 1, 0)
        grad_gate = (grad_hidden * up * sigmoid_gate * (1.0 + gate * (1.0 - sigmoid_gate))).astype(BF)
        grad_up = (grad_hidden * silu).astype(BF)
        back_parts[i] = dot(grad_gate, w_gate, 1, 0) + dot(grad_up, w_up, 1, 0)
        if i == last:
            tied = tick(back_parts[i], *gate_grads[1:], *up_grads[1:], *hiddens[1:], grad_gate, grad_up, hidden)
            back_parts[i], gate_grads[1:], up_grads[1:], hiddens[1:] = tied[0], tied[1:4], tied[4:7], tied[7:10]
            grad_gate, grad_up, hidden = tied[10:]
        back_parts[i] = fold_core(back_parts[i])
        hiddens[i], gate_grads[i], up_grads[i] = hidden, grad_gate, grad_up

    def over_chunks(left, right):
        return sum(dot(left[i], right[i], 0, 0) for i in range(4)).astype(BF)

    back_hops = [None] * 4

    def send_back(i):
        back_hops[i] = hop(back_parts[i].astype(BF), ORDER[i]).astype(F32)

    send_back(first)
    gate_grad = over_chunks(gate_grads, ff_chunks)
    gate_grad, *up_grads, back_parts[third], back_parts[second] = tick(
        gate_grad, *up_grads, back_parts[third], back_parts[second]
    )
    back_parts[third] = fold_plane(back_parts[third], "x")
    send_back(second)
    up_grad = over_chunks(up_grads, ff_chunks)
    up_grad, *hiddens, back_parts[last], back_parts[third] = tick(up_grad, *hiddens, back_parts[last], back_parts[third])
    back_parts[last] = fold_plane(back_parts[last], "x")
    send_back(third)
    gu_own, gu_other = split(jnp.stack([gate_grad, up_grad]), 1, y)
    gu_other = swap(gu_other, "y")
    mlp_parts = [dot(item, down, 1, 1).astype(BF) for item in hiddens]
    mlp_parts = [fold_core(item) for item in mlp_parts]
    down_grad = over_chunks(cot_chunks, hiddens)
    down_own, down_other = split(down_grad, 1, y)
    back_parts[last], down_other, *mlp_parts = tick(back_parts[last], down_other, *mlp_parts)
    down_other = swap(down_other, "y")
    mlp_parts = [fold_plane(item, "x") for item in mlp_parts]
    back_parts[last], *back_hops[1:], mlp_parts[0], mlp_parts[1] = tick(
        back_parts[last], *back_hops[1:], mlp_parts[0], mlp_parts[1]
    )
    grad_normed_two = back_parts[last] + back_hops[1] + back_hops[2] + back_hops[3]

    grad_norm_two, grad_gain_two = rms_back(grad_normed_two, residual, scale_two, gain_two)
    grad_residual = cotangent[0].astype(F32) + grad_norm_two
    grad_branch = grad_residual.astype(BF)
    grad_attended = dot(grad_branch, out_full, 1, 0).astype(BF)
    grad_slots = reorder(to_slots_kernel, place, grad_attended, (16, BLK, 128))
    pieces = send_hops(grad_slots.reshape(4, 2, 2, BLK, 128))
    pieces, *mlp_parts = tick(pieces, *mlp_parts)
    mlp_hops = [mlp_parts[0]] + [hop(item.astype(BF), j) for j, item in zip(ORDER[1:], mlp_parts[1:])]
    pieces = send_core(send_plane(pieces, "y"))
    grad_proj = attend_back(place, saved, pieces, cosine, sine).reshape(16 * BLK, 384)
    back_parts = [fold_core(dot(grad_proj[j * quarter : (j + 1) * quarter], heads_qkv, 1, 0)) for j in range(4)]
    qkv_grad = dot(grad_proj, normed_all, 0, 0)
    qkv_own, qkv_other = split(qkv_grad.reshape(3, 2 * HD, width), 1, x)
    tied = tick(*back_parts, qkv_other.astype(BF), grad_branch, gu_other, down_other, *mlp_hops)
    back_parts, (qkv_other, grad_branch, gu_other, down_other), mlp_hops = list(tied[:4]), tied[4:8], tied[8:]
    qkv_other = swap(qkv_other, "x")
    back_parts = [fold_plane(item, "y") for item in back_parts]
    gu_moved = lax.ppermute((gu_own.astype(F32) + gu_other.astype(F32)).astype(BF), AXES, perm_of(ff_place))
    down_moved = lax.ppermute((down_own.astype(F32) + down_other.astype(F32)).astype(BF), AXES, perm_of(ff_place))
    branch_hops = [grad_branch] + [hop(grad_branch, j) for j in ORDER[1:]]
    back_parts[first], branch_hops[1] = tick(back_parts[first], branch_hops[1])
    send_back(first)
    back_parts[second], branch_hops[2], qkv_other = tick(back_parts[second], branch_hops[2], qkv_other)
    send_back(second)
    qkv_moved = lax.ppermute((qkv_own + qkv_other.astype(F32)).astype(BF), AXES, perm_of(attn_place))
    back_parts[third], branch_hops[3], down_moved = tick(back_parts[third], branch_hops[3], down_moved)
    send_back(third)
    branch_others = [swap(item, "y") for item in branch_hops]
    branch_chunks = [with_partner(*item) for item in zip(branch_hops, branch_others)]
    back_hops[3], gu_moved, qkv_grad, *mlp_hops = tick(back_hops[3], gu_moved, qkv_grad, *mlp_hops)
    mlp_term = mlp_hops[0] + sum(item.astype(F32) for item in mlp_hops[1:])
    layer_out = (residual + mlp_term).astype(BF)
    gain_part = jnp.sum(qkv_grad * heads_qkv.astype(F32), axis=0) / gain_one
    low_chunks = low_slots.reshape(4, quarter, 128)
    out_grad = sum(dot(item, low_chunks[i], 0, 0) for i, item in enumerate(branch_chunks))
    out_own, out_other = split(out_grad, 1, x)
    grad_out_proj = move(out_own + swap(out_other.astype(BF), "x").astype(F32), attn_place)
    grad_normed_one = back_parts[last] + back_hops[1] + back_hops[2] + back_hops[3]
    grad_qkv = jnp.transpose(qkv_moved.astype(F32), (1, 0, 2))
    grad_gate_up = jnp.transpose(gu_moved.astype(F32), (1, 0, 2))
    grad_down = down_moved.astype(F32)

    weighted = grad_normed_one * gain_one
    inner_mean = jnp.mean(weighted * inputs, axis=-1, keepdims=True)
    grad_input = grad_residual + scale_one * weighted - inputs * scale_one**3 * inner_mean

    gains = jnp.stack([gain_part, grad_gain_two])
    for name, bit in (("y", y), ("x", x)):
        mine, other = split(gains, 1, bit)
        gains = mine + swap(other, name)
    size = gains.shape[1] // 4
    quarters = [lax.dynamic_slice_in_dim(gains, (z ^ j) * size, size, 1) for j in range(4)]
    gains = quarters[0] + hop(quarters[1], 1) + hop(quarters[2], 2) + hop(quarters[3], 3)
    mine, other = split(gains, 1, c)
    gains = mine + swap(other, "c")
    return (
        layer_out[None],
        grad_input[None],
        gains[0],
        gains[1],
        grad_qkv,
        grad_out_proj,
        grad_gate_up,
        grad_down,
    )


def solution(mesh):
    if mesh.shape["fsdp"] != 4 or mesh.shape["seq"] != 8:
        return general_solution(mesh)
    fine = Mesh(mesh.devices.reshape(2, 2, 4, 2), AXES)
    fsdp, seq = ("y", "x"), ("z", "c")
    tokens = P(fsdp, seq, None)
    return jax.shard_map(
        body,
        mesh=fine,
        in_specs=(
            tokens,
            P(),
            P(),
            P(fsdp, None, None),
            P(fsdp, None),
            P(fsdp, None, None),
            P(fsdp, None),
            tokens,
        ),
        out_specs=(
            tokens,
            tokens,
            P(fsdp + seq),
            P(fsdp + seq),
            P(seq + fsdp, None, None),
            P(None, seq + fsdp),
            P(seq + fsdp, None, None),
            P(None, seq + fsdp),
        ),
        check_vma=False,
    )
```

```python
import functools
import math

import jax
import jax.numpy as jnp
from jax import lax
from jax.experimental import pallas as pl
from jax.experimental.pallas import tpu as pltpu
from jax.sharding import Mesh
from jax.sharding import PartitionSpec as P

HD = 64


NORM_EPS = 1e-05
ROPE_BASE = 130000.0


def rotate(matrix):
    shaped = matrix.reshape(matrix.shape[:-1] + (matrix.shape[-1] // HD, 2, HD // 2))
    turned = jnp.stack([-shaped[..., 1, :], shaped[..., 0, :]], axis=-2)
    return turned.reshape(matrix.shape)


def rotate_back(matrix):
    shaped = matrix.reshape(matrix.shape[:-1] + (matrix.shape[-1] // HD, 2, HD // 2))
    turned = jnp.stack([shaped[..., 1, :], -shaped[..., 0, :]], axis=-2)
    return turned.reshape(matrix.shape)


def rope_tables(positions, columns):
    freq_index = (jnp.arange(columns, dtype=jnp.int32) % (HD // 2)).astype(jnp.float32)
    inverse = ROPE_BASE ** (-2.0 * freq_index / HD)
    angles = positions.astype(jnp.float32)[:, None] * inverse[None, :]
    return (jnp.cos(angles), jnp.sin(angles))


def rms_scale(matrix):
    return lax.rsqrt(jnp.mean(matrix * matrix, axis=-1, keepdims=True) + NORM_EPS)


def rms_back(grad_normed, matrix, scale_rows, gain):
    weighted = grad_normed * gain
    inner_mean = jnp.mean(weighted * matrix, axis=-1, keepdims=True)
    grad_matrix = scale_rows * weighted - matrix * scale_rows**3 * inner_mean
    grad_gain = jnp.sum(grad_normed * matrix * scale_rows, axis=0)
    return (grad_matrix, grad_gain)


def attend_forward(queries, key_rows, values):
    seq_count, length, width_here = queries.shape
    heads_here = width_here // HD
    q_block = min(512, length)
    k_block = min(256, length)
    inv_root = 1.0 / math.sqrt(HD)
    shaped_q = queries.reshape(seq_count, length, heads_here, HD)
    shaped_k = key_rows.reshape(seq_count, length, heads_here, HD)
    shaped_v = values.reshape(seq_count, length, heads_here, HD)

    def query_step(q_index, carried):
        attended, totals = carried
        offset = q_index * q_block
        q_rows = lax.dynamic_slice_in_dim(shaped_q, offset, q_block, 1)
        query_pos = offset + jnp.arange(q_block, dtype=jnp.int32)

        def key_step(k_index, running):
            unnorm, denominator = running
            k_start = k_index * k_block
            k_rows = lax.dynamic_slice_in_dim(shaped_k, k_start, k_block, 1)
            v_rows = lax.dynamic_slice_in_dim(shaped_v, k_start, k_block, 1)
            scores = (
                jnp.einsum("bqhd,bkhd->bhqk", q_rows, k_rows, preferred_element_type=jnp.float32)
                * inv_root
            )
            causal = (k_start + jnp.arange(k_block, dtype=jnp.int32))[None, :] <= query_pos[:, None]
            exp_scores = jnp.where(causal, jnp.exp(scores), 0.0)
            denominator = denominator + jnp.sum(exp_scores, axis=-1)
            unnorm = unnorm + jnp.einsum(
                "bhqk,bkhd->bqhd",
                exp_scores.astype(jnp.bfloat16),
                v_rows,
                preferred_element_type=jnp.float32,
            )
            return (unnorm, denominator)

        start_state = (
            jnp.zeros((seq_count, q_block, heads_here, HD), jnp.float32),
            jnp.zeros((seq_count, heads_here, q_block), jnp.float32),
        )
        unnorm, denominator = lax.fori_loop(0, (offset + q_block) // k_block, key_step, start_state)
        block_out = unnorm / jnp.transpose(denominator, (0, 2, 1))[..., None]
        attended = lax.dynamic_update_slice_in_dim(attended, block_out, offset, 1)
        totals = lax.dynamic_update_slice_in_dim(totals, denominator, offset, 2)
        return (attended, totals)

    initial = (
        jnp.zeros((seq_count, length, heads_here, HD), jnp.float32),
        jnp.zeros((seq_count, heads_here, length), jnp.float32),
    )
    attended, totals = lax.fori_loop(0, length // q_block, query_step, initial)
    return (attended.reshape(seq_count, length, width_here), totals)


def attend_backward(queries, key_rows, values, attended, totals, grad_attended):
    seq_count, length, width_here = queries.shape
    heads_here = width_here // HD
    q_block = min(512, length)
    k_block = min(256, length)
    inv_root = 1.0 / math.sqrt(HD)
    shaped_q = queries.reshape(seq_count, length, heads_here, HD)
    shaped_k = key_rows.reshape(seq_count, length, heads_here, HD)
    shaped_v = values.reshape(seq_count, length, heads_here, HD)
    shaped_grad = grad_attended.reshape(seq_count, length, heads_here, HD).astype(jnp.float32)
    shaped_att = attended.reshape(seq_count, length, heads_here, HD)
    totals_rows = jnp.transpose(totals, (0, 2, 1))
    grad_total = -jnp.sum(shaped_grad * shaped_att, axis=-1) / totals_rows
    grad_unnorm = (shaped_grad / totals_rows[..., None]).astype(jnp.bfloat16)

    def query_step(q_index, carried):
        grad_q, grad_k, grad_v = carried
        offset = q_index * q_block
        q_rows = lax.dynamic_slice_in_dim(shaped_q, offset, q_block, 1)
        g_rows = lax.dynamic_slice_in_dim(grad_unnorm, offset, q_block, 1)
        total_rows = jnp.transpose(
            lax.dynamic_slice_in_dim(grad_total, offset, q_block, 1), (0, 2, 1)
        )
        query_pos = offset + jnp.arange(q_block, dtype=jnp.int32)

        def key_step(k_index, running):
            dq_acc, dk_all, dv_all = running
            k_start = k_index * k_block
            k_rows = lax.dynamic_slice_in_dim(shaped_k, k_start, k_block, 1)
            v_rows = lax.dynamic_slice_in_dim(shaped_v, k_start, k_block, 1)
            scores = (
                jnp.einsum("bqhd,bkhd->bhqk", q_rows, k_rows, preferred_element_type=jnp.float32)
                * inv_root
            )
            causal = (k_start + jnp.arange(k_block, dtype=jnp.int32))[None, :] <= query_pos[:, None]
            exp_scores = jnp.where(causal, jnp.exp(scores), 0.0)
            grad_prob = jnp.einsum(
                "bqhd,bkhd->bhqk", g_rows, v_rows, preferred_element_type=jnp.float32
            )
            grad_scores = (exp_scores * (grad_prob + total_rows[..., None])).astype(jnp.bfloat16)
            dq_acc = (
                dq_acc
                + jnp.einsum(
                    "bhqk,bkhd->bqhd", grad_scores, k_rows, preferred_element_type=jnp.float32
                )
                * inv_root
            )
            dk_part = (
                jnp.einsum(
                    "bhqk,bqhd->bkhd", grad_scores, q_rows, preferred_element_type=jnp.float32
                )
                * inv_root
            )
            dv_part = jnp.einsum(
                "bhqk,bqhd->bkhd",
                exp_scores.astype(jnp.bfloat16),
                g_rows,
                preferred_element_type=jnp.float32,
            )
            dk_slice = lax.dynamic_slice_in_dim(dk_all, k_start, k_block, 1) + dk_part
            dv_slice = lax.dynamic_slice_in_dim(dv_all, k_start, k_block, 1) + dv_part
            dk_all = lax.dynamic_update_slice_in_dim(dk_all, dk_slice, k_start, 1)
            dv_all = lax.dynamic_update_slice_in_dim(dv_all, dv_slice, k_start, 1)
            return (dq_acc, dk_all, dv_all)

        start_state = (jnp.zeros((seq_count, q_block, heads_here, HD), jnp.float32), grad_k, grad_v)
        dq_block, grad_k, grad_v = lax.fori_loop(
            0, (offset + q_block) // k_block, key_step, start_state
        )
        grad_q = lax.dynamic_update_slice_in_dim(grad_q, dq_block, offset, 1)
        return (grad_q, grad_k, grad_v)

    empty = jnp.zeros((seq_count, length, heads_here, HD), jnp.float32)
    grad_q, grad_k, grad_v = lax.fori_loop(0, length // q_block, query_step, (empty, empty, empty))
    cosine, sine_table = rope_tables(jnp.arange(length, dtype=jnp.int32), width_here)
    grad_q = grad_q.reshape(seq_count, length, width_here)
    grad_k = grad_k.reshape(seq_count, length, width_here)
    grad_v = grad_v.reshape(seq_count, length, width_here)
    raw_q = grad_q * cosine + rotate_back(grad_q * sine_table)
    raw_k = grad_k * cosine + rotate_back(grad_k * sine_table)
    return jnp.stack([raw_q, raw_k, grad_v]).astype(jnp.bfloat16)


def general_body(residual_in, attn_gain, mlp_gain, w_qkv, w_out, w_gate_up, w_down, cotangent):
    seq_count, shard_len, model_width = residual_in.shape
    tokens = seq_count * shard_len
    seq_index = lax.axis_index("seq")
    positions = seq_index * shard_len + jnp.arange(tokens, dtype=jnp.int32) % shard_len
    cosine, sine_table = rope_tables(positions, model_width)
    inputs = residual_in.reshape(tokens, model_width).astype(jnp.float32)
    gain_one = attn_gain.astype(jnp.float32)
    gain_two = mlp_gain.astype(jnp.float32)
    scale_one = rms_scale(inputs)
    normed_one = (inputs * scale_one * gain_one).astype(jnp.bfloat16)
    qkv_full, out_full = (
        lax.all_gather(w_qkv, "fsdp", axis=0, tiled=True),
        lax.all_gather(w_out, "fsdp", axis=0, tiled=True),
    )
    projected = jnp.einsum("td,fpd->ptf", normed_one, qkv_full, preferred_element_type=jnp.float32)
    queries = (projected[0] * cosine + rotate(projected[0]) * sine_table).astype(jnp.bfloat16)
    key_rows = (projected[1] * cosine + rotate(projected[1]) * sine_table).astype(jnp.bfloat16)
    values = projected[2].astype(jnp.bfloat16)
    stacked = jnp.stack([queries, key_rows, values]).reshape(3, seq_count, shard_len, model_width)
    head_view = lax.all_to_all(stacked, "seq", split_axis=3, concat_axis=2, tiled=True)
    attended, totals = attend_forward(head_view[0], head_view[1], head_view[2])
    attended_heads = attended.astype(jnp.bfloat16)
    sent_back = lax.all_to_all(attended_heads, "seq", split_axis=1, concat_axis=2, tiled=True)
    attended_low = sent_back.reshape(tokens, model_width)
    branch = jnp.einsum("ti,fi->tf", attended_low, out_full, preferred_element_type=jnp.float32)
    residual = inputs + branch
    scale_two = rms_scale(residual)
    normed_two = (residual * scale_two * gain_two).astype(jnp.bfloat16)
    up_full, down_full = (
        lax.all_gather(w_gate_up, "fsdp", axis=0, tiled=True),
        lax.all_gather(w_down, "fsdp", axis=0, tiled=True),
    )
    gate_up = jnp.einsum("td,jpd->ptj", normed_two, up_full, preferred_element_type=jnp.float32)
    hidden = (jax.nn.silu(gate_up[0]) * gate_up[1]).astype(jnp.bfloat16)
    mlp_term = jnp.einsum("tj,fj->tf", hidden, down_full, preferred_element_type=jnp.float32)
    layer_out = (
        (residual + mlp_term).astype(jnp.bfloat16).reshape(seq_count, shard_len, model_width)
    )
    grad_out = cotangent.reshape(tokens, model_width)
    up_again, down_again = (
        lax.all_gather(w_gate_up, "fsdp", axis=0, tiled=True),
        lax.all_gather(w_down, "fsdp", axis=0, tiled=True),
    )
    grad_hidden = jnp.einsum("tf,fj->tj", grad_out, down_again, preferred_element_type=jnp.float32)
    sigmoid_gate = jax.nn.sigmoid(gate_up[0])
    grad_gate = grad_hidden * gate_up[1] * sigmoid_gate * (1.0 + gate_up[0] * (1.0 - sigmoid_gate))
    grad_up = grad_hidden * jax.nn.silu(gate_up[0])
    grad_gu = jnp.stack([grad_gate, grad_up]).astype(jnp.bfloat16)
    grad_normed_two = jnp.einsum(
        "ptj,jpd->td", grad_gu, up_again, preferred_element_type=jnp.float32
    )
    ff_width = grad_gu.shape[2]
    unit_rows = jnp.concatenate([grad_gu, hidden[None]], axis=0).reshape(
        3, seq_count, shard_len, ff_width
    )
    unit_cols = lax.all_to_all(unit_rows, "seq", split_axis=3, concat_axis=2, tiled=True)
    normed_piece = lax.all_gather(
        normed_two.reshape(seq_count, shard_len, model_width), "seq", axis=1, tiled=True
    )
    grad_piece = lax.all_gather(cotangent, "seq", axis=1, tiled=True)
    gu_part = jnp.einsum(
        "psnj,snd->jpd", unit_cols[:2], normed_piece, preferred_element_type=jnp.float32
    )
    down_part = jnp.einsum(
        "snf,snj->fj", grad_piece, unit_cols[2], preferred_element_type=jnp.float32
    )
    gu_part, down_part = (gu_part, down_part)
    grad_gate_up, grad_down = (
        lax.psum_scatter(
            gu_part.astype(jnp.bfloat16), "fsdp", scatter_dimension=0, tiled=True
        ).astype(jnp.float32),
        lax.psum_scatter(
            down_part.astype(jnp.bfloat16), "fsdp", scatter_dimension=1, tiled=True
        ).astype(jnp.float32),
    )
    grad_norm_two, grad_gain_two = rms_back(grad_normed_two, residual, scale_two, gain_two)
    grad_residual = grad_out.astype(jnp.float32) + grad_norm_two
    qkv_back, out_back = (
        lax.all_gather(w_qkv, "fsdp", axis=0, tiled=True),
        lax.all_gather(w_out, "fsdp", axis=0, tiled=True),
    )
    grad_branch = grad_residual.astype(jnp.bfloat16)
    grad_attended = jnp.einsum(
        "tf,fi->ti", grad_branch, out_back, preferred_element_type=jnp.float32
    )
    grad_attended = grad_attended.astype(jnp.bfloat16).reshape(seq_count, shard_len, model_width)
    grad_heads = lax.all_to_all(grad_attended, "seq", split_axis=2, concat_axis=1, tiled=True)
    grad_stacked = attend_backward(
        head_view[0], head_view[1], head_view[2], attended, totals, grad_heads
    )
    normed_piece = lax.all_gather(
        normed_one.reshape(seq_count, shard_len, model_width), "seq", axis=1, tiled=True
    )
    branch_piece = lax.all_gather(
        grad_branch.reshape(seq_count, shard_len, model_width), "seq", axis=1, tiled=True
    )
    grad_piece = grad_stacked
    qkv_part = jnp.einsum(
        "psnf,snd->fpd", grad_piece, normed_piece, preferred_element_type=jnp.float32
    )
    out_part = jnp.einsum(
        "snf,sni->fi", branch_piece, attended_heads, preferred_element_type=jnp.float32
    )
    qkv_part, out_part = (qkv_part, out_part)
    grad_qkv, grad_out_proj = (
        lax.psum_scatter(
            qkv_part.astype(jnp.bfloat16), "fsdp", scatter_dimension=0, tiled=True
        ).astype(jnp.float32),
        lax.psum_scatter(
            out_part.astype(jnp.bfloat16), "fsdp", scatter_dimension=1, tiled=True
        ).astype(jnp.float32),
    )
    grad_projected = lax.all_to_all(grad_stacked, "seq", split_axis=2, concat_axis=3, tiled=True)
    grad_projected = grad_projected.reshape(3, tokens, model_width)
    grad_normed_one = jnp.einsum(
        "ptf,fpd->td", grad_projected, qkv_back, preferred_element_type=jnp.float32
    )
    grad_norm_one, grad_gain_one = rms_back(grad_normed_one, inputs, scale_one, gain_one)
    grad_input = (grad_residual + grad_norm_one).reshape(seq_count, shard_len, model_width)
    grad_attn_gain, grad_mlp_gain = (
        lax.psum_scatter(grad_gain_one, ("fsdp", "seq"), scatter_dimension=0, tiled=True),
        lax.psum_scatter(grad_gain_two, ("fsdp", "seq"), scatter_dimension=0, tiled=True),
    )
    return (
        layer_out,
        grad_input,
        grad_attn_gain,
        grad_mlp_gain,
        grad_qkv,
        grad_out_proj,
        grad_gate_up,
        grad_down,
    )


def general_solution(mesh):
    return jax.shard_map(
        general_body,
        mesh=mesh,
        in_specs=(
            P("fsdp", "seq", None),
            P(),
            P(),
            P("fsdp", None, None),
            P("fsdp", None),
            P("fsdp", None, None),
            P("fsdp", None),
            P("fsdp", "seq", None),
        ),
        out_specs=(
            P("fsdp", "seq", None),
            P("fsdp", "seq", None),
            P(("fsdp", "seq")),
            P(("fsdp", "seq")),
            P(("seq", "fsdp"), None, None),
            P(None, ("seq", "fsdp")),
            P(("seq", "fsdp"), None, None),
            P(None, ("seq", "fsdp")),
        ),
        check_vma=False,
    )


BF = jnp.bfloat16
F32 = jnp.float32
AXES = ("y", "x", "z", "c")
PAIR = [(0, 1), (1, 0)]
BLK = 128
ORDER = (0, 1, 3, 2)
Q_ROWS = 256


def swap(value, axis):
    return lax.ppermute(value, axis, PAIR)


def hop(value, dist):
    return lax.ppermute(value, "z", [(i, i ^ dist) for i in range(4)])


def tick(*values):
    return lax.optimization_barrier(values)


def with_partner(held, other):
    both = jnp.concatenate([held, other], axis=0)
    return jnp.concatenate([both, swap(both, "c")], axis=0)


def fold_core(part):
    n = part.shape[0] // 2
    return part[:n].astype(F32) + swap(part[n:].astype(BF), "c").astype(F32)


def fold_plane(kept, plane):
    n = kept.shape[0] // 2
    return kept[:n] + swap(kept[n:].astype(BF), plane).astype(F32)


def fold_hops(parts):
    total = parts[0]
    for j, part in zip(ORDER[1:], parts[1:]):
        total = total + hop(part.astype(BF), j).astype(F32)
    return total


def send_core(pieces):
    return jnp.stack([pieces[:, 0], swap(pieces[:, 1], "c")], axis=1)


def send_plane(pieces, plane):
    return jnp.stack([pieces[:, :, 0], swap(pieces[:, :, 1], plane)], axis=2)


def send_hops(pieces):
    return jnp.stack([hop(pieces[i], j) if j else pieces[i] for i, j in enumerate(ORDER)])


def turn(value, back):
    lane = lax.broadcasted_iota(jnp.int32, value.shape, 1) % HD
    up = pltpu.roll(value, HD // 2, 1)
    down = pltpu.roll(value, value.shape[1] - HD // 2, 1)
    return jnp.where(lane < HD // 2, down, -up) if back else jnp.where(lane < HD // 2, -down, up)


def head_mask(value, head):
    lane = lax.broadcasted_iota(jnp.int32, value.shape, 1)
    return jnp.where((lane < HD) == (head == 0), value, jnp.zeros_like(value))


def dot(left, right, left_dim, right_dim):
    return lax.dot_general(
        left, right, (((left_dim,), (right_dim,)), ((), ())), preferred_element_type=F32
    )


def causal_exp(scores, start):
    rows, cols = scores.shape
    query = start + lax.broadcasted_iota(jnp.int32, (rows, rows), 0)
    key = cols - rows + lax.broadcasted_iota(jnp.int32, (rows, rows), 1)
    last = jnp.where(key <= query, jnp.exp(scores[:, cols - rows :]), 0.0)
    if cols == rows:
        return last
    return jnp.concatenate([jnp.exp(scores[:, : cols - rows]), last], axis=1)


def chunk_of(slot):
    dist = slot >> 1
    return dist ^ (dist >> 1)


def attend_kernel(place, proj, cosine, sine, q_out, k_out, v_out, att_out, den_out, low_out):
    length = q_out.shape[1]
    me = place[0]
    for block in range(length // BLK):
        slot = me ^ block
        here = proj[chunk_of(slot), slot & 1, 0]
        rows = slice(block * BLK, (block + 1) * BLK)
        cos_rows, sin_rows = cosine[rows, :], sine[rows, :]
        raw_q, raw_k = here[:, :128], here[:, 128:256]
        q_out[0, rows, :] = (raw_q * cos_rows + turn(raw_q, False) * sin_rows).astype(BF)
        k_out[0, rows, :] = (raw_k * cos_rows + turn(raw_k, False) * sin_rows).astype(BF)
        v_out[0, rows, :] = here[:, 256:].astype(BF)
    for start in range(0, length, Q_ROWS):
        seen = start + Q_ROWS
        queries = q_out[0, start:seen, :] * jnp.asarray(0.125, BF)
        keys, values = k_out[0, :seen, :], v_out[0, :seen, :]
        unnorm, den = None, None
        for head in range(2):
            exp_scores = causal_exp(dot(head_mask(queries, head), keys, 1, 1), start)
            total = jnp.sum(exp_scores, axis=1, keepdims=True)
            part = dot(exp_scores.astype(BF), head_mask(values, head), 1, 0)
            total = head_mask(jnp.broadcast_to(total, part.shape), head)
            unnorm = part if unnorm is None else unnorm + part
            den = total if den is None else den + total
        attended = unnorm / den
        att_out[0, start:seen, :] = attended
        den_out[0, start:seen, :] = den
        for block in range(start // BLK, seen // BLK):
            slot = me ^ block
            first = block * BLK - start
            low_out[chunk_of(slot), slot & 1, 0] = attended[first : first + BLK].astype(BF)


def attend_back_kernel(
    place, q_ref, k_ref, v_ref, att_ref, den_ref, grad_ref, cosine, sine, out, grad, grad_q, grad_k, grad_v
):
    length = q_ref.shape[1]
    me = place[0]
    for block in range(length // BLK):
        slot = me ^ block
        grad[block * BLK : (block + 1) * BLK, :] = grad_ref[chunk_of(slot), slot & 1, 0].astype(F32)
    grad_k[...] = jnp.zeros_like(grad_k)
    grad_v[...] = jnp.zeros_like(grad_v)
    for start in range(0, length, Q_ROWS):
        seen = start + Q_ROWS
        queries = q_ref[0, start:seen, :] * jnp.asarray(0.125, BF)
        keys, values = k_ref[0, :seen, :], v_ref[0, :seen, :]
        grad_rows, den = grad[start:seen, :], den_ref[0, start:seen, :]
        unnorm = (grad_rows / den).astype(BF)
        weighted = grad_rows * att_ref[0, start:seen, :] / den
        total_q = None
        for head in range(2):
            q_head, g_head = head_mask(queries, head), head_mask(unnorm, head)
            exp_scores = causal_exp(dot(q_head, keys, 1, 1), start)
            grad_total = -jnp.sum(head_mask(weighted, head), axis=1, keepdims=True)
            grad_scores = (exp_scores * (dot(g_head, values, 1, 1) + grad_total)).astype(BF)
            part = dot(grad_scores, head_mask(keys, head), 1, 0)
            total_q = part if total_q is None else total_q + part
            grad_k[:seen, :] += dot(grad_scores, q_head, 0, 0)
            grad_v[:seen, :] += dot(exp_scores.astype(BF), g_head, 0, 0)
        grad_q[start:seen, :] = total_q * 0.125
    for block in range(length // BLK):
        slot = me ^ block
        rows = slice(block * BLK, (block + 1) * BLK)
        cos_rows, sin_rows = cosine[rows, :], sine[rows, :]
        for part, held in enumerate((grad_q, grad_k)):
            value = held[rows, :]
            raw = value * cos_rows + turn(value * sin_rows, True)
            out[chunk_of(slot), slot & 1, 0, :, part * 128 : (part + 1) * 128] = raw.astype(BF)
        out[chunk_of(slot), slot & 1, 0, :, 256:] = grad_v[rows, :].astype(BF)


def whole(shape):
    return pl.BlockSpec(shape, lambda i, place: (0,) * len(shape))


def per_seq(shape, at):
    return pl.BlockSpec(shape, lambda i, place: tuple(i if d == at else 0 for d in range(len(shape))))


def attend(place, proj, cosine, sine):
    length = cosine.shape[0]
    seq = jax.ShapeDtypeStruct((2, length, 128), BF)
    wide = jax.ShapeDtypeStruct((2, length, 128), F32)
    return pl.pallas_call(
        attend_kernel,
        grid_spec=pltpu.PrefetchScalarGridSpec(
            num_scalar_prefetch=1,
            grid=(2,),
            in_specs=[per_seq((4, 2, 1, BLK, 384), 2), whole((length, 128)), whole((length, 128))],
            out_specs=[per_seq((1, length, 128), 0)] * 5 + [per_seq((4, 2, 1, BLK, 128), 2)],
        ),
        out_shape=[seq, seq, seq, wide, wide, jax.ShapeDtypeStruct((4, 2, 2, BLK, 128), BF)],
        compiler_params=pltpu.CompilerParams(vmem_limit_bytes=40 << 20),
        cost_estimate=pl.CostEstimate(flops=0, bytes_accessed=1 << 20, transcendentals=0),
        name="attend",
    )(place, proj, cosine, sine)


def attend_back(place, saved, grad_slots, cosine, sine):
    length = cosine.shape[0]
    return pl.pallas_call(
        attend_back_kernel,
        grid_spec=pltpu.PrefetchScalarGridSpec(
            num_scalar_prefetch=1,
            grid=(2,),
            in_specs=[per_seq((1, length, 128), 0)] * 5
            + [per_seq((4, 2, 1, BLK, 128), 2), whole((length, 128)), whole((length, 128))],
            out_specs=per_seq((4, 2, 1, BLK, 384), 2),
            scratch_shapes=[pltpu.VMEM((length, 128), F32)] * 4,
        ),
        out_shape=jax.ShapeDtypeStruct((4, 2, 2, BLK, 384), BF),
        compiler_params=pltpu.CompilerParams(vmem_limit_bytes=40 << 20),
        cost_estimate=pl.CostEstimate(flops=0, bytes_accessed=1 << 20, transcendentals=0),
        name="attend_back",
    )(place, *saved, grad_slots, cosine, sine)


def perm_of(target):
    pairs = []
    for index in range(32):
        bits = [(index >> shift) & 1 for shift in (4, 3, 2, 1, 0)]
        place = 0
        for bit in target(*bits):
            place = 2 * place + bit
        pairs.append((index, place))
    return pairs


def join_kernel(place, pair, far, pair_c, far_c, out):
    cols = pair.shape[1]
    early = pl.program_id(0) < 2
    for core in range(2):
        here, there = slice(core * cols, (core + 1) * cols), slice((1 - core) * cols, (2 - core) * cols)

        @pl.when((place[3] == core) & early)
        def _():
            out[:, here] = pair[...]
            out[:, there] = pair_c[...]

        @pl.when((place[3] == core) & jnp.logical_not(early))
        def _():
            out[:, here] = far[...]
            out[:, there] = far_c[...]


def join_out(place, pair, far, pair_c, far_c):
    rows, cols = pair.shape[0] // 2, pair.shape[1]
    early = pl.BlockSpec((rows, cols), lambda i, place: (jnp.minimum(i, 1), 0))
    late = pl.BlockSpec((rows, cols), lambda i, place: (jnp.maximum(i - 2, 0), 0))
    return pl.pallas_call(
        join_kernel,
        grid_spec=pltpu.PrefetchScalarGridSpec(
            num_scalar_prefetch=1,
            grid=(4,),
            in_specs=[early, late, early, late],
            out_specs=pl.BlockSpec(
                (rows, 2 * cols), lambda i, place: (place[2] ^ (((i & 1) << 1) | (i >> 1)), 0)
            ),
        ),
        out_shape=jax.ShapeDtypeStruct((4 * rows, 2 * cols), BF),
        cost_estimate=pl.CostEstimate(flops=0, bytes_accessed=1 << 20, transcendentals=0),
        name="join_out",
    )(place, pair, far, pair_c, far_c)


def order_kernel(place, block, out):
    out[...] = block[...]


def order_rows(place, value):
    rows, cols = value.shape[0] // 4, value.shape[1]
    return pl.pallas_call(
        order_kernel,
        grid_spec=pltpu.PrefetchScalarGridSpec(
            num_scalar_prefetch=1,
            grid=(4,),
            in_specs=[pl.BlockSpec((rows, cols), lambda i, place: (i, 0))],
            out_specs=pl.BlockSpec((rows, cols), lambda i, place: (place[2] ^ i, 0)),
        ),
        out_shape=jax.ShapeDtypeStruct(value.shape, BF),
        cost_estimate=pl.CostEstimate(flops=0, bytes_accessed=1 << 20, transcendentals=0),
        name="order_rows",
    )(place, value)


def slot_of(rel):
    bit_y, bit_z0, bit_c, bit_z1 = rel >> 3, (rel >> 2) & 1, (rel >> 1) & 1, rel & 1
    return ORDER.index(2 * bit_z1 + bit_z0) * 4 + bit_c * 2 + bit_y


def to_heads_kernel(place, slots, out):
    for rel in range(16):
        pair = place[1] ^ rel
        out[:, pl.ds(pl.multiple_of(pair * 128, 128), 128)] = slots[slot_of(rel)]


def to_slots_kernel(place, rows, out):
    for rel in range(16):
        pair = place[1] ^ rel
        out[slot_of(rel)] = rows[:, pl.ds(pl.multiple_of(pair * 128, 128), 128)]


def reorder(kernel, place, value, shape):
    return pl.pallas_call(
        kernel,
        in_specs=[pl.BlockSpec(memory_space=pltpu.SMEM), pl.BlockSpec(memory_space=pltpu.VMEM)],
        out_specs=pl.BlockSpec(memory_space=pltpu.VMEM),
        out_shape=jax.ShapeDtypeStruct(shape, BF),
        cost_estimate=pl.CostEstimate(flops=0, bytes_accessed=1 << 20, transcendentals=0),
        name=kernel.__name__,
    )(place, value)


def split(value, dim, bit):
    size = value.shape[dim] // 2
    return (
        lax.dynamic_slice_in_dim(value, bit * size, size, dim),
        lax.dynamic_slice_in_dim(value, (1 - bit) * size, size, dim),
    )


def ff_place(at_y, at_x, at_z1, at_z0, at_c):
    return at_y, at_z0, at_z1, at_x, at_c


def attn_place(at_y, at_x, at_z1, at_z0, at_c):
    return at_z1, at_x, at_y, at_z0, at_c


def move(value, target):
    return lax.ppermute(value.astype(BF), AXES, perm_of(target)).astype(F32)


def ff_step(value, name, leaving):
    flip = 8 if name == "x" else 2
    pairs = [(i, i ^ flip) for i in range(32) if (((i >> 3) ^ (i >> 1)) & 1) == leaving]
    return lax.ppermute(value, AXES, pairs)


def body(residual_in, attn_gain, mlp_gain, w_qkv, w_out, w_gate_up, w_down, cotangent):
    y, x, z, c = [lax.axis_index(name) for name in AXES]
    z1, z0 = z >> 1, z & 1
    group, part = 2 * y + x, 2 * z + c
    width = residual_in.shape[2]
    length = BLK * 8
    quarter = 4 * BLK
    units = w_gate_up.shape[0] // 8
    inputs = residual_in[0].astype(F32)
    gain_one, gain_two = attn_gain.astype(F32), mlp_gain.astype(F32)
    scale_one = rms_scale(inputs)
    normed_one = (inputs * scale_one * gain_one).astype(BF)

    qkv_sent = lax.dynamic_slice_in_dim(w_qkv, (4 * c + 2 * z1) * HD, 2 * HD, 0)
    qkv_sent = jnp.transpose(qkv_sent, (1, 0, 2)).reshape(3 * 2 * HD, width)
    x_pairs = [((i & 1) * 4 + i, (1 - (i & 1)) * 4 + i) for i in range(4)]
    y_pairs = [((i >> 1) * 4 + i, (1 - (i >> 1)) * 4 + i) for i in range(4)]
    hops = [normed_one] + [hop(normed_one, j) for j in ORDER[1:]]
    others = [swap(normed_one, "y")]
    qkv_moved = lax.ppermute(qkv_sent, ("x", "z"), x_pairs)
    cols = width // 2
    out_own = lax.dynamic_slice_in_dim(w_out, c * cols, cols, 1)
    hops[3], qkv_moved = tick(hops[3], qkv_moved)
    others += [swap(held, "y") for held in hops[1:]]
    normed_all = jnp.concatenate([with_partner(*item) for item in zip(hops, others)], axis=0)
    heads_qkv = jnp.where(x == z0, qkv_sent, qkv_moved)

    def columns(side):
        first = (8 * (2 * z1 + side) + 4 * c + z0) * units
        return jnp.concatenate(
            [lax.dynamic_slice_in_dim(w_down, first + 2 * j * units, units, 1) for j in range(2)], axis=1
        )

    gu_sent = [lax.dynamic_slice_in_dim(w_gate_up, (4 * c + 2 * j + z0) * units, units, 0) for j in range(2)]
    gate_sent = [jnp.reshape(item[:, 0], (units, width)) for item in gu_sent]
    up_sent = [jnp.reshape(item[:, 1], (units, width)) for item in gu_sent]
    down_own, down_sent = columns(x), columns(1 - x)

    def to_y(value):
        return lax.ppermute(value, ("y", "z"), y_pairs)

    cos_half, sin_half = rope_tables(jnp.arange(length, dtype=jnp.int32), HD // 2)
    cosine, sine = jnp.tile(cos_half, (1, 4)), jnp.tile(sin_half, (1, 4))
    place = jnp.stack([part, 8 * y + 4 * z0 + 2 * c + z1, group, c]).astype(jnp.int32)

    *firsts, cot, out_own, down_sent, down_own = tick(
        normed_all, heads_qkv, *gate_sent, *up_sent, cosine, sine, place, cotangent[0], out_own, down_sent, down_own
    )
    normed_all, heads_qkv, gate_sent, up_sent = firsts[0], firsts[1], firsts[2:4], firsts[4:6]
    cosine, sine, place = firsts[6:]
    cot_hops = [cot, hop(cot, 1), hop(cot, 3), None]
    cot_others = [swap(cot, "x")]
    down_x = swap(down_sent, "x")
    out_y = swap(out_own, "y")

    proj = dot(normed_all, heads_qkv, 1, 1)
    *saved, low_slots = attend(place, proj.reshape(4, 2, 2, BLK, 384), cosine, sine)
    pieces = send_core(low_slots)
    pieces, out_y, cot_hops[1], cot_others[0], down_x = tick(pieces, out_y, cot_hops[1], cot_others[0], down_x)
    out_pair = jnp.concatenate([out_own, out_y], axis=0)
    out_x = swap(out_pair, "x")
    down_pair = jnp.concatenate([down_own, down_x], axis=0)
    down_y = swap(down_pair, "y")
    pair_c = swap(out_pair, "c")
    pieces = send_plane(pieces, "y")
    pieces, cot_hops[2] = tick(pieces, cot_hops[2])
    pieces = send_hops(pieces)
    pieces, out_x, down_y, gate_sent[0], cot, pair_c = tick(pieces, out_x, down_y, gate_sent[0], cot, pair_c)
    cot_hops[3] = hop(cot, 2)
    gate_moved = [to_y(gate_sent[0])]
    attended = reorder(to_heads_kernel, place, pieces.reshape(16, BLK, 128), (BLK, width))
    out_full = join_out(place, out_pair, out_x, pair_c, swap(out_x, "c"))
    attended, out_full, cot_hops[1], cot_hops[2] = tick(attended, out_full, cot_hops[1], cot_hops[2])
    cot_others += [swap(item, "x") for item in cot_hops[1:3]]
    residual = inputs + dot(attended, out_full, 1, 1)
    scale_two = rms_scale(residual)
    normed_two = (residual * scale_two * gain_two).astype(BF)

    normed_two, cot_hops[3], gate_moved[0], gate_sent[1], down_pair, down_y, cot_hops[0], cot_others[0] = tick(
        normed_two, cot_hops[3], gate_moved[0], gate_sent[1], down_pair, down_y, cot_hops[0], cot_others[0]
    )
    gate_moved.append(to_y(gate_sent[1]))
    hops = [normed_two] + [hop(normed_two, j) for j in ORDER[1:]]
    others = [swap(normed_two, "x")]
    hops[1], gate_moved[1], up_sent[0], cot_others[1] = tick(hops[1], gate_moved[1], up_sent[0], cot_others[1])
    up_moved = [to_y(up_sent[0])]
    others.append(swap(hops[1], "x"))
    hops[2], up_moved[0], up_sent[1], cot_others[2], cot_hops[3] = tick(
        hops[2], up_moved[0], up_sent[1], cot_others[2], cot_hops[3]
    )
    up_moved.append(to_y(up_sent[1]))
    others.append(swap(hops[2], "x"))
    cot_others.append(swap(cot_hops[3], "x"))
    others.append(swap(hops[3], "x"))
    w_gate, w_up = [
        jnp.concatenate([jnp.where(y == z1, own, moved) for own, moved in zip(held, arrived)], axis=0)
        for held, arrived in ((gate_sent, gate_moved), (up_sent, up_moved))
    ]
    down = order_rows(place, jnp.concatenate([down_pair, down_y], axis=0))
    ff_chunks = [with_partner(*item) for item in zip(hops, others)]
    cot_chunks = [with_partner(*item) for item in zip(cot_hops, cot_others)]

    hiddens, gate_grads, up_grads, back_parts, mlp_parts = [[None] * 4 for _ in range(5)]
    first, second, third, last = turns = (2, 3, 1, 0)
    for i in turns:
        if i == third:
            ff_chunks[i], back_parts[first] = tick(ff_chunks[i], back_parts[first])
            back_parts[first] = fold_plane(back_parts[first], "x")
        if i == last:
            ff_chunks[i], back_parts[second], back_parts[first], mlp_parts[first] = tick(
                ff_chunks[i], back_parts[second], back_parts[first], mlp_parts[first]
            )
            mlp_parts[first] = fold_plane(mlp_parts[first], "x")
            back_parts[second] = fold_plane(back_parts[second], "x")
        gate, up = dot(ff_chunks[i], w_gate, 1, 1), dot(ff_chunks[i], w_up, 1, 1)
        sigmoid_gate = jax.nn.sigmoid(gate)
        silu = gate * sigmoid_gate
        hidden = (silu * up).astype(BF)
        grad_hidden = dot(cot_chunks[i], down, 1, 0)
        grad_gate = (grad_hidden * up * sigmoid_gate * (1.0 + gate * (1.0 - sigmoid_gate))).astype(BF)
        grad_up = (grad_hidden * silu).astype(BF)
        back_parts[i] = dot(grad_gate, w_gate, 1, 0) + dot(grad_up, w_up, 1, 0)
        if i == last:
            tied = tick(back_parts[i], *gate_grads[1:], *up_grads[1:], *hiddens[1:], grad_gate, grad_up, hidden)
            back_parts[i], gate_grads[1:], up_grads[1:], hiddens[1:] = tied[0], tied[1:4], tied[4:7], tied[7:10]
            grad_gate, grad_up, hidden = tied[10:]
        back_parts[i] = fold_core(back_parts[i])
        mlp_parts[i] = fold_core(dot(hidden, down, 1, 1))
        hiddens[i], gate_grads[i], up_grads[i] = hidden, grad_gate, grad_up

    def over_chunks(left, right):
        return sum(dot(left[i], right[i], 0, 0) for i in range(4)).astype(BF)

    back_hops = [None] * 4

    def send_back(i):
        back_hops[i] = hop(back_parts[i].astype(BF), ORDER[i])

    send_back(first)
    gate_grad = over_chunks(gate_grads, ff_chunks)
    gate_grad, *up_grads, back_parts[third], back_parts[second], mlp_parts[second], mlp_parts[first] = tick(
        gate_grad, *up_grads, back_parts[third], back_parts[second], mlp_parts[second], mlp_parts[first]
    )
    mlp_parts[second] = fold_plane(mlp_parts[second], "x")
    back_parts[third] = fold_plane(back_parts[third], "x")
    send_back(second)
    gate_own, gate_other = split(gate_grad, 0, y)
    gate_other = swap(gate_other, "y")
    up_grad = over_chunks(up_grads, ff_chunks)
    up_grad, *hiddens, back_parts[last], back_parts[third], mlp_parts[third], gate_other = tick(
        up_grad, *hiddens, back_parts[last], back_parts[third], mlp_parts[third], gate_other
    )
    mlp_parts[third] = fold_plane(mlp_parts[third], "x")
    back_parts[last] = fold_plane(back_parts[last], "x")
    send_back(third)
    up_own, up_other = split(up_grad, 0, y)
    up_other = swap(up_other, "y")
    down_grad = over_chunks(cot_chunks, hiddens)
    down_own, down_other = split(down_grad, 1, y)
    back_parts[last], down_other, mlp_parts[last], mlp_parts[second] = tick(
        back_parts[last], down_other, mlp_parts[last], mlp_parts[second]
    )
    mlp_parts[last] = fold_plane(mlp_parts[last], "x")
    mlp_hops = [None] + [hop(mlp_parts[i].astype(BF), ORDER[i]) for i in (1, 2, 3)]
    back_parts[last], *back_hops[1:], up_other, down_other = tick(
        back_parts[last], *back_hops[1:], up_other, down_other
    )
    down_other = swap(down_other, "y")
    grad_normed_two = back_parts[last] + back_hops[1] + back_hops[2] + back_hops[3]

    grad_norm_two, grad_gain_two = rms_back(grad_normed_two, residual, scale_two, gain_two)
    grad_residual = cotangent[0].astype(F32) + grad_norm_two
    grad_branch = grad_residual.astype(BF)
    grad_attended = dot(grad_branch, out_full, 1, 0).astype(BF)
    grad_slots = reorder(to_slots_kernel, place, grad_attended, (16, BLK, 128))
    pieces = send_hops(grad_slots.reshape(4, 2, 2, BLK, 128))
    pieces, mlp_hops[first], grad_branch, down_other, gate_other, up_other = tick(
        pieces, mlp_hops[first], grad_branch, down_other, gate_other, up_other
    )
    gate_sum = (gate_own.astype(F32) + gate_other.astype(F32)).astype(BF)
    up_sum = (up_own.astype(F32) + up_other.astype(F32)).astype(BF)
    gate_step, up_step = ff_step(gate_sum, "x", 1), ff_step(up_sum, "z", 1)
    branch_hops = [grad_branch] + [hop(grad_branch, j) for j in ORDER[1:]]
    pieces = send_core(send_plane(pieces, "y"))
    grad_proj = attend_back(place, saved, pieces, cosine, sine).reshape(16 * BLK, 384)
    back_parts = [fold_core(dot(grad_proj[j * quarter : (j + 1) * quarter], heads_qkv, 1, 0)) for j in range(4)]
    qkv_grad = dot(grad_proj, normed_all, 0, 0)
    qkv_own, qkv_other = split(qkv_grad.reshape(3, 2 * HD, width), 1, x)
    *back_parts, qkv_other, mlp_hops[second] = tick(*back_parts, qkv_other.astype(BF), mlp_hops[second])
    qkv_other = swap(qkv_other, "x")
    back_parts = [fold_plane(item, "y") for item in back_parts]
    down_sum = (down_own.astype(F32) + down_other.astype(F32)).astype(BF)
    half = down_sum.shape[0] // 2
    down_steps = [ff_step(down_sum[:half], "x", 1), ff_step(down_sum[half:], "z", 1)]
    back_parts[first], branch_hops[1], branch_hops[2] = tick(back_parts[first], branch_hops[1], branch_hops[2])
    send_back(first)
    back_parts[second], branch_hops[3], qkv_other, mlp_hops[third], gate_step, up_step = tick(
        back_parts[second], branch_hops[3], qkv_other, mlp_hops[third], gate_step, up_step
    )
    send_back(second)
    gate_step, up_step = ff_step(gate_step, "z", 0), ff_step(up_step, "x", 0)
    qkv_moved = lax.ppermute((qkv_own + qkv_other.astype(F32)).astype(BF), AXES, perm_of(attn_place))
    back_parts[third], back_parts[last], back_hops[first], down_steps[0], down_steps[1], *branch_hops = tick(
        back_parts[third], back_parts[last], back_hops[first], *down_steps, *branch_hops
    )
    down_steps = [ff_step(down_steps[0], "z", 0), ff_step(down_steps[1], "x", 0)]
    send_back(third)
    branch_others = [swap(item, "y") for item in branch_hops]
    branch_others[0], back_hops[second], mlp_parts[last], qkv_grad, gate_step, up_step = tick(
        branch_others[0], back_hops[second], mlp_parts[last], qkv_grad, gate_step, up_step
    )
    branch_chunks = [with_partner(*item) for item in zip(branch_hops, branch_others)]
    mlp_term = mlp_parts[last] + sum(item.astype(F32) for item in mlp_hops[1:])
    layer_out = (residual + mlp_term).astype(BF)
    gain_part = jnp.sum(qkv_grad * heads_qkv.astype(F32), axis=0) / gain_one
    low_chunks = low_slots.reshape(4, quarter, 128)
    out_grad = sum(dot(item, low_chunks[i], 0, 0) for i, item in enumerate(branch_chunks))
    out_own, out_other = split(out_grad, 1, x)
    grad_out_proj = move(out_own + swap(out_other.astype(BF), "x").astype(F32), attn_place)
    grad_normed_one = back_parts[last] + back_hops[1] + back_hops[2] + back_hops[3]
    grad_qkv = jnp.transpose(qkv_moved.astype(F32), (1, 0, 2))
    stays = x == z0
    grad_gate_up = jnp.stack([jnp.where(stays, gate_sum, gate_step), jnp.where(stays, up_sum, up_step)], axis=1).astype(F32)
    grad_down = jnp.where(stays, down_sum, jnp.concatenate(down_steps, axis=0)).astype(F32)

    weighted = grad_normed_one * gain_one
    inner_mean = jnp.mean(weighted * inputs, axis=-1, keepdims=True)
    grad_input = grad_residual + scale_one * weighted - inputs * scale_one**3 * inner_mean

    gains = jnp.stack([gain_part, grad_gain_two])
    for name, bit in (("y", y), ("x", x)):
        mine, other = split(gains, 1, bit)
        gains = mine + swap(other, name)
    size = gains.shape[1] // 4
    quarters = [lax.dynamic_slice_in_dim(gains, (z ^ j) * size, size, 1) for j in range(4)]
    gains = quarters[0] + hop(quarters[1], 1) + hop(quarters[2], 2) + hop(quarters[3], 3)
    mine, other = split(gains, 1, c)
    gains = mine + swap(other, "c")
    return (
        layer_out[None],
        grad_input[None],
        gains[0],
        gains[1],
        grad_qkv,
        grad_out_proj,
        grad_gate_up,
        grad_down,
    )


def solution(mesh):
    if mesh.shape["fsdp"] != 4 or mesh.shape["seq"] != 8:
        return general_solution(mesh)
    fine = Mesh(mesh.devices.reshape(2, 2, 4, 2), AXES)
    fsdp, seq = ("y", "x"), ("z", "c")
    tokens = P(fsdp, seq, None)
    return jax.shard_map(
        body,
        mesh=fine,
        in_specs=(
            tokens,
            P(),
            P(),
            P(fsdp, None, None),
            P(fsdp, None),
            P(fsdp, None, None),
            P(fsdp, None),
            tokens,
        ),
        out_specs=(
            tokens,
            tokens,
            P(fsdp + seq),
            P(fsdp + seq),
            P(seq + fsdp, None, None),
            P(None, seq + fsdp),
            P(seq + fsdp, None, None),
            P(None, seq + fsdp),
        ),
        check_vma=False,
    )
```

```python
import functools
import math

import jax
import jax.numpy as jnp
from jax import lax
from jax.experimental import pallas as pl
from jax.experimental.pallas import tpu as pltpu
from jax.sharding import Mesh
from jax.sharding import PartitionSpec as P

HD = 64


NORM_EPS = 1e-05
ROPE_BASE = 130000.0


def rotate(matrix):
    shaped = matrix.reshape(matrix.shape[:-1] + (matrix.shape[-1] // HD, 2, HD // 2))
    turned = jnp.stack([-shaped[..., 1, :], shaped[..., 0, :]], axis=-2)
    return turned.reshape(matrix.shape)


def rotate_back(matrix):
    shaped = matrix.reshape(matrix.shape[:-1] + (matrix.shape[-1] // HD, 2, HD // 2))
    turned = jnp.stack([shaped[..., 1, :], -shaped[..., 0, :]], axis=-2)
    return turned.reshape(matrix.shape)


def rope_tables(positions, columns):
    freq_index = (jnp.arange(columns, dtype=jnp.int32) % (HD // 2)).astype(jnp.float32)
    inverse = ROPE_BASE ** (-2.0 * freq_index / HD)
    angles = positions.astype(jnp.float32)[:, None] * inverse[None, :]
    return (jnp.cos(angles), jnp.sin(angles))


def rms_scale(matrix):
    return lax.rsqrt(jnp.mean(matrix * matrix, axis=-1, keepdims=True) + NORM_EPS)


def rms_back(grad_normed, matrix, scale_rows, gain):
    weighted = grad_normed * gain
    inner_mean = jnp.mean(weighted * matrix, axis=-1, keepdims=True)
    grad_matrix = scale_rows * weighted - matrix * scale_rows**3 * inner_mean
    grad_gain = jnp.sum(grad_normed * matrix * scale_rows, axis=0)
    return (grad_matrix, grad_gain)


def attend_forward(queries, key_rows, values):
    seq_count, length, width_here = queries.shape
    heads_here = width_here // HD
    q_block = min(512, length)
    k_block = min(256, length)
    inv_root = 1.0 / math.sqrt(HD)
    shaped_q = queries.reshape(seq_count, length, heads_here, HD)
    shaped_k = key_rows.reshape(seq_count, length, heads_here, HD)
    shaped_v = values.reshape(seq_count, length, heads_here, HD)

    def query_step(q_index, carried):
        attended, totals = carried
        offset = q_index * q_block
        q_rows = lax.dynamic_slice_in_dim(shaped_q, offset, q_block, 1)
        query_pos = offset + jnp.arange(q_block, dtype=jnp.int32)

        def key_step(k_index, running):
            unnorm, denominator = running
            k_start = k_index * k_block
            k_rows = lax.dynamic_slice_in_dim(shaped_k, k_start, k_block, 1)
            v_rows = lax.dynamic_slice_in_dim(shaped_v, k_start, k_block, 1)
            scores = (
                jnp.einsum("bqhd,bkhd->bhqk", q_rows, k_rows, preferred_element_type=jnp.float32)
                * inv_root
            )
            causal = (k_start + jnp.arange(k_block, dtype=jnp.int32))[None, :] <= query_pos[:, None]
            exp_scores = jnp.where(causal, jnp.exp(scores), 0.0)
            denominator = denominator + jnp.sum(exp_scores, axis=-1)
            unnorm = unnorm + jnp.einsum(
                "bhqk,bkhd->bqhd",
                exp_scores.astype(jnp.bfloat16),
                v_rows,
                preferred_element_type=jnp.float32,
            )
            return (unnorm, denominator)

        start_state = (
            jnp.zeros((seq_count, q_block, heads_here, HD), jnp.float32),
            jnp.zeros((seq_count, heads_here, q_block), jnp.float32),
        )
        unnorm, denominator = lax.fori_loop(0, (offset + q_block) // k_block, key_step, start_state)
        block_out = unnorm / jnp.transpose(denominator, (0, 2, 1))[..., None]
        attended = lax.dynamic_update_slice_in_dim(attended, block_out, offset, 1)
        totals = lax.dynamic_update_slice_in_dim(totals, denominator, offset, 2)
        return (attended, totals)

    initial = (
        jnp.zeros((seq_count, length, heads_here, HD), jnp.float32),
        jnp.zeros((seq_count, heads_here, length), jnp.float32),
    )
    attended, totals = lax.fori_loop(0, length // q_block, query_step, initial)
    return (attended.reshape(seq_count, length, width_here), totals)


def attend_backward(queries, key_rows, values, attended, totals, grad_attended):
    seq_count, length, width_here = queries.shape
    heads_here = width_here // HD
    q_block = min(512, length)
    k_block = min(256, length)
    inv_root = 1.0 / math.sqrt(HD)
    shaped_q = queries.reshape(seq_count, length, heads_here, HD)
    shaped_k = key_rows.reshape(seq_count, length, heads_here, HD)
    shaped_v = values.reshape(seq_count, length, heads_here, HD)
    shaped_grad = grad_attended.reshape(seq_count, length, heads_here, HD).astype(jnp.float32)
    shaped_att = attended.reshape(seq_count, length, heads_here, HD)
    totals_rows = jnp.transpose(totals, (0, 2, 1))
    grad_total = -jnp.sum(shaped_grad * shaped_att, axis=-1) / totals_rows
    grad_unnorm = (shaped_grad / totals_rows[..., None]).astype(jnp.bfloat16)

    def query_step(q_index, carried):
        grad_q, grad_k, grad_v = carried
        offset = q_index * q_block
        q_rows = lax.dynamic_slice_in_dim(shaped_q, offset, q_block, 1)
        g_rows = lax.dynamic_slice_in_dim(grad_unnorm, offset, q_block, 1)
        total_rows = jnp.transpose(
            lax.dynamic_slice_in_dim(grad_total, offset, q_block, 1), (0, 2, 1)
        )
        query_pos = offset + jnp.arange(q_block, dtype=jnp.int32)

        def key_step(k_index, running):
            dq_acc, dk_all, dv_all = running
            k_start = k_index * k_block
            k_rows = lax.dynamic_slice_in_dim(shaped_k, k_start, k_block, 1)
            v_rows = lax.dynamic_slice_in_dim(shaped_v, k_start, k_block, 1)
            scores = (
                jnp.einsum("bqhd,bkhd->bhqk", q_rows, k_rows, preferred_element_type=jnp.float32)
                * inv_root
            )
            causal = (k_start + jnp.arange(k_block, dtype=jnp.int32))[None, :] <= query_pos[:, None]
            exp_scores = jnp.where(causal, jnp.exp(scores), 0.0)
            grad_prob = jnp.einsum(
                "bqhd,bkhd->bhqk", g_rows, v_rows, preferred_element_type=jnp.float32
            )
            grad_scores = (exp_scores * (grad_prob + total_rows[..., None])).astype(jnp.bfloat16)
            dq_acc = (
                dq_acc
                + jnp.einsum(
                    "bhqk,bkhd->bqhd", grad_scores, k_rows, preferred_element_type=jnp.float32
                )
                * inv_root
            )
            dk_part = (
                jnp.einsum(
                    "bhqk,bqhd->bkhd", grad_scores, q_rows, preferred_element_type=jnp.float32
                )
                * inv_root
            )
            dv_part = jnp.einsum(
                "bhqk,bqhd->bkhd",
                exp_scores.astype(jnp.bfloat16),
                g_rows,
                preferred_element_type=jnp.float32,
            )
            dk_slice = lax.dynamic_slice_in_dim(dk_all, k_start, k_block, 1) + dk_part
            dv_slice = lax.dynamic_slice_in_dim(dv_all, k_start, k_block, 1) + dv_part
            dk_all = lax.dynamic_update_slice_in_dim(dk_all, dk_slice, k_start, 1)
            dv_all = lax.dynamic_update_slice_in_dim(dv_all, dv_slice, k_start, 1)
            return (dq_acc, dk_all, dv_all)

        start_state = (jnp.zeros((seq_count, q_block, heads_here, HD), jnp.float32), grad_k, grad_v)
        dq_block, grad_k, grad_v = lax.fori_loop(
            0, (offset + q_block) // k_block, key_step, start_state
        )
        grad_q = lax.dynamic_update_slice_in_dim(grad_q, dq_block, offset, 1)
        return (grad_q, grad_k, grad_v)

    empty = jnp.zeros((seq_count, length, heads_here, HD), jnp.float32)
    grad_q, grad_k, grad_v = lax.fori_loop(0, length // q_block, query_step, (empty, empty, empty))
    cosine, sine_table = rope_tables(jnp.arange(length, dtype=jnp.int32), width_here)
    grad_q = grad_q.reshape(seq_count, length, width_here)
    grad_k = grad_k.reshape(seq_count, length, width_here)
    grad_v = grad_v.reshape(seq_count, length, width_here)
    raw_q = grad_q * cosine + rotate_back(grad_q * sine_table)
    raw_k = grad_k * cosine + rotate_back(grad_k * sine_table)
    return jnp.stack([raw_q, raw_k, grad_v]).astype(jnp.bfloat16)


def general_body(residual_in, attn_gain, mlp_gain, w_qkv, w_out, w_gate_up, w_down, cotangent):
    seq_count, shard_len, model_width = residual_in.shape
    tokens = seq_count * shard_len
    seq_index = lax.axis_index("seq")
    positions = seq_index * shard_len + jnp.arange(tokens, dtype=jnp.int32) % shard_len
    cosine, sine_table = rope_tables(positions, model_width)
    inputs = residual_in.reshape(tokens, model_width).astype(jnp.float32)
    gain_one = attn_gain.astype(jnp.float32)
    gain_two = mlp_gain.astype(jnp.float32)
    scale_one = rms_scale(inputs)
    normed_one = (inputs * scale_one * gain_one).astype(jnp.bfloat16)
    qkv_full, out_full = (
        lax.all_gather(w_qkv, "fsdp", axis=0, tiled=True),
        lax.all_gather(w_out, "fsdp", axis=0, tiled=True),
    )
    projected = jnp.einsum("td,fpd->ptf", normed_one, qkv_full, preferred_element_type=jnp.float32)
    queries = (projected[0] * cosine + rotate(projected[0]) * sine_table).astype(jnp.bfloat16)
    key_rows = (projected[1] * cosine + rotate(projected[1]) * sine_table).astype(jnp.bfloat16)
    values = projected[2].astype(jnp.bfloat16)
    stacked = jnp.stack([queries, key_rows, values]).reshape(3, seq_count, shard_len, model_width)
    head_view = lax.all_to_all(stacked, "seq", split_axis=3, concat_axis=2, tiled=True)
    attended, totals = attend_forward(head_view[0], head_view[1], head_view[2])
    attended_heads = attended.astype(jnp.bfloat16)
    sent_back = lax.all_to_all(attended_heads, "seq", split_axis=1, concat_axis=2, tiled=True)
    attended_low = sent_back.reshape(tokens, model_width)
    branch = jnp.einsum("ti,fi->tf", attended_low, out_full, preferred_element_type=jnp.float32)
    residual = inputs + branch
    scale_two = rms_scale(residual)
    normed_two = (residual * scale_two * gain_two).astype(jnp.bfloat16)
    up_full, down_full = (
        lax.all_gather(w_gate_up, "fsdp", axis=0, tiled=True),
        lax.all_gather(w_down, "fsdp", axis=0, tiled=True),
    )
    gate_up = jnp.einsum("td,jpd->ptj", normed_two, up_full, preferred_element_type=jnp.float32)
    hidden = (jax.nn.silu(gate_up[0]) * gate_up[1]).astype(jnp.bfloat16)
    mlp_term = jnp.einsum("tj,fj->tf", hidden, down_full, preferred_element_type=jnp.float32)
    layer_out = (
        (residual + mlp_term).astype(jnp.bfloat16).reshape(seq_count, shard_len, model_width)
    )
    grad_out = cotangent.reshape(tokens, model_width)
    up_again, down_again = (
        lax.all_gather(w_gate_up, "fsdp", axis=0, tiled=True),
        lax.all_gather(w_down, "fsdp", axis=0, tiled=True),
    )
    grad_hidden = jnp.einsum("tf,fj->tj", grad_out, down_again, preferred_element_type=jnp.float32)
    sigmoid_gate = jax.nn.sigmoid(gate_up[0])
    grad_gate = grad_hidden * gate_up[1] * sigmoid_gate * (1.0 + gate_up[0] * (1.0 - sigmoid_gate))
    grad_up = grad_hidden * jax.nn.silu(gate_up[0])
    grad_gu = jnp.stack([grad_gate, grad_up]).astype(jnp.bfloat16)
    grad_normed_two = jnp.einsum(
        "ptj,jpd->td", grad_gu, up_again, preferred_element_type=jnp.float32
    )
    ff_width = grad_gu.shape[2]
    unit_rows = jnp.concatenate([grad_gu, hidden[None]], axis=0).reshape(
        3, seq_count, shard_len, ff_width
    )
    unit_cols = lax.all_to_all(unit_rows, "seq", split_axis=3, concat_axis=2, tiled=True)
    normed_piece = lax.all_gather(
        normed_two.reshape(seq_count, shard_len, model_width), "seq", axis=1, tiled=True
    )
    grad_piece = lax.all_gather(cotangent, "seq", axis=1, tiled=True)
    gu_part = jnp.einsum(
        "psnj,snd->jpd", unit_cols[:2], normed_piece, preferred_element_type=jnp.float32
    )
    down_part = jnp.einsum(
        "snf,snj->fj", grad_piece, unit_cols[2], preferred_element_type=jnp.float32
    )
    gu_part, down_part = (gu_part, down_part)
    grad_gate_up, grad_down = (
        lax.psum_scatter(
            gu_part.astype(jnp.bfloat16), "fsdp", scatter_dimension=0, tiled=True
        ).astype(jnp.float32),
        lax.psum_scatter(
            down_part.astype(jnp.bfloat16), "fsdp", scatter_dimension=1, tiled=True
        ).astype(jnp.float32),
    )
    grad_norm_two, grad_gain_two = rms_back(grad_normed_two, residual, scale_two, gain_two)
    grad_residual = grad_out.astype(jnp.float32) + grad_norm_two
    qkv_back, out_back = (
        lax.all_gather(w_qkv, "fsdp", axis=0, tiled=True),
        lax.all_gather(w_out, "fsdp", axis=0, tiled=True),
    )
    grad_branch = grad_residual.astype(jnp.bfloat16)
    grad_attended = jnp.einsum(
        "tf,fi->ti", grad_branch, out_back, preferred_element_type=jnp.float32
    )
    grad_attended = grad_attended.astype(jnp.bfloat16).reshape(seq_count, shard_len, model_width)
    grad_heads = lax.all_to_all(grad_attended, "seq", split_axis=2, concat_axis=1, tiled=True)
    grad_stacked = attend_backward(
        head_view[0], head_view[1], head_view[2], attended, totals, grad_heads
    )
    normed_piece = lax.all_gather(
        normed_one.reshape(seq_count, shard_len, model_width), "seq", axis=1, tiled=True
    )
    branch_piece = lax.all_gather(
        grad_branch.reshape(seq_count, shard_len, model_width), "seq", axis=1, tiled=True
    )
    grad_piece = grad_stacked
    qkv_part = jnp.einsum(
        "psnf,snd->fpd", grad_piece, normed_piece, preferred_element_type=jnp.float32
    )
    out_part = jnp.einsum(
        "snf,sni->fi", branch_piece, attended_heads, preferred_element_type=jnp.float32
    )
    qkv_part, out_part = (qkv_part, out_part)
    grad_qkv, grad_out_proj = (
        lax.psum_scatter(
            qkv_part.astype(jnp.bfloat16), "fsdp", scatter_dimension=0, tiled=True
        ).astype(jnp.float32),
        lax.psum_scatter(
            out_part.astype(jnp.bfloat16), "fsdp", scatter_dimension=1, tiled=True
        ).astype(jnp.float32),
    )
    grad_projected = lax.all_to_all(grad_stacked, "seq", split_axis=2, concat_axis=3, tiled=True)
    grad_projected = grad_projected.reshape(3, tokens, model_width)
    grad_normed_one = jnp.einsum(
        "ptf,fpd->td", grad_projected, qkv_back, preferred_element_type=jnp.float32
    )
    grad_norm_one, grad_gain_one = rms_back(grad_normed_one, inputs, scale_one, gain_one)
    grad_input = (grad_residual + grad_norm_one).reshape(seq_count, shard_len, model_width)
    grad_attn_gain, grad_mlp_gain = (
        lax.psum_scatter(grad_gain_one, ("fsdp", "seq"), scatter_dimension=0, tiled=True),
        lax.psum_scatter(grad_gain_two, ("fsdp", "seq"), scatter_dimension=0, tiled=True),
    )
    return (
        layer_out,
        grad_input,
        grad_attn_gain,
        grad_mlp_gain,
        grad_qkv,
        grad_out_proj,
        grad_gate_up,
        grad_down,
    )


def general_solution(mesh):
    return jax.shard_map(
        general_body,
        mesh=mesh,
        in_specs=(
            P("fsdp", "seq", None),
            P(),
            P(),
            P("fsdp", None, None),
            P("fsdp", None),
            P("fsdp", None, None),
            P("fsdp", None),
            P("fsdp", "seq", None),
        ),
        out_specs=(
            P("fsdp", "seq", None),
            P("fsdp", "seq", None),
            P(("fsdp", "seq")),
            P(("fsdp", "seq")),
            P(("seq", "fsdp"), None, None),
            P(None, ("seq", "fsdp")),
            P(("seq", "fsdp"), None, None),
            P(None, ("seq", "fsdp")),
        ),
        check_vma=False,
    )


BF = jnp.bfloat16
F32 = jnp.float32
AXES = ("y", "x", "z", "c")
PAIR = [(0, 1), (1, 0)]
BLK = 128
ORDER = (0, 1, 3, 2)
Q_ROWS = 256


def swap(value, axis):
    return lax.ppermute(value, axis, PAIR)


def hop(value, dist):
    return lax.ppermute(value, "z", [(i, i ^ dist) for i in range(4)])


def tick(*values):
    return lax.optimization_barrier(values)


def with_partner(held, other):
    both = jnp.concatenate([held, other], axis=0)
    return jnp.concatenate([both, swap(both, "c")], axis=0)


def fold_core(part):
    n = part.shape[0] // 2
    return part[:n].astype(F32) + swap(part[n:].astype(BF), "c").astype(F32)


def fold_plane(kept, plane):
    n = kept.shape[0] // 2
    return kept[:n] + swap(kept[n:].astype(BF), plane).astype(F32)


def fold_hops(parts):
    total = parts[0]
    for j, part in zip(ORDER[1:], parts[1:]):
        total = total + hop(part.astype(BF), j).astype(F32)
    return total


def send_core(pieces):
    return jnp.stack([pieces[:, 0], swap(pieces[:, 1], "c")], axis=1)


def send_plane(pieces, plane):
    return jnp.stack([pieces[:, :, 0], swap(pieces[:, :, 1], plane)], axis=2)


def send_hops(pieces):
    return jnp.stack([hop(pieces[i], j) if j else pieces[i] for i, j in enumerate(ORDER)])


def turn(value, back):
    lane = lax.broadcasted_iota(jnp.int32, value.shape, 1) % HD
    up = pltpu.roll(value, HD // 2, 1)
    down = pltpu.roll(value, value.shape[1] - HD // 2, 1)
    return jnp.where(lane < HD // 2, down, -up) if back else jnp.where(lane < HD // 2, -down, up)


def head_mask(value, head):
    lane = lax.broadcasted_iota(jnp.int32, value.shape, 1)
    return jnp.where((lane < HD) == (head == 0), value, jnp.zeros_like(value))


def dot(left, right, left_dim, right_dim):
    return lax.dot_general(
        left, right, (((left_dim,), (right_dim,)), ((), ())), preferred_element_type=F32
    )


def causal_exp(scores, start):
    rows, cols = scores.shape
    query = start + lax.broadcasted_iota(jnp.int32, (rows, rows), 0)
    key = cols - rows + lax.broadcasted_iota(jnp.int32, (rows, rows), 1)
    last = jnp.where(key <= query, jnp.exp(scores[:, cols - rows :]), 0.0)
    if cols == rows:
        return last
    return jnp.concatenate([jnp.exp(scores[:, : cols - rows]), last], axis=1)


def chunk_of(slot):
    dist = slot >> 1
    return dist ^ (dist >> 1)


def attend_kernel(place, proj, cosine, sine, q_out, k_out, v_out, att_out, den_out, low_out):
    length = q_out.shape[1]
    me = place[0]
    for block in range(length // BLK):
        slot = me ^ block
        here = proj[chunk_of(slot), slot & 1, 0]
        rows = slice(block * BLK, (block + 1) * BLK)
        cos_rows, sin_rows = cosine[rows, :], sine[rows, :]
        raw_q, raw_k = here[:, :128], here[:, 128:256]
        q_out[0, rows, :] = (raw_q * cos_rows + turn(raw_q, False) * sin_rows).astype(BF)
        k_out[0, rows, :] = (raw_k * cos_rows + turn(raw_k, False) * sin_rows).astype(BF)
        v_out[0, rows, :] = here[:, 256:].astype(BF)
    for start in range(0, length, Q_ROWS):
        seen = start + Q_ROWS
        queries = q_out[0, start:seen, :] * jnp.asarray(0.125, BF)
        keys, values = k_out[0, :seen, :], v_out[0, :seen, :]
        unnorm, den = None, None
        for head in range(2):
            exp_scores = causal_exp(dot(head_mask(queries, head), keys, 1, 1), start)
            total = jnp.sum(exp_scores, axis=1, keepdims=True)
            part = dot(exp_scores.astype(BF), head_mask(values, head), 1, 0)
            total = head_mask(jnp.broadcast_to(total, part.shape), head)
            unnorm = part if unnorm is None else unnorm + part
            den = total if den is None else den + total
        attended = unnorm / den
        att_out[0, start:seen, :] = attended
        den_out[0, start:seen, :] = den
        for block in range(start // BLK, seen // BLK):
            slot = me ^ block
            first = block * BLK - start
            low_out[chunk_of(slot), slot & 1, 0] = attended[first : first + BLK].astype(BF)


def attend_back_kernel(
    place, q_ref, k_ref, v_ref, att_ref, den_ref, grad_ref, cosine, sine, out, grad, grad_q, grad_k, grad_v
):
    length = q_ref.shape[1]
    me = place[0]
    for block in range(length // BLK):
        slot = me ^ block
        grad[block * BLK : (block + 1) * BLK, :] = grad_ref[chunk_of(slot), slot & 1, 0].astype(F32)
    grad_k[...] = jnp.zeros_like(grad_k)
    grad_v[...] = jnp.zeros_like(grad_v)
    for start in range(0, length, Q_ROWS):
        seen = start + Q_ROWS
        queries = q_ref[0, start:seen, :] * jnp.asarray(0.125, BF)
        keys, values = k_ref[0, :seen, :], v_ref[0, :seen, :]
        grad_rows, den = grad[start:seen, :], den_ref[0, start:seen, :]
        unnorm = (grad_rows / den).astype(BF)
        weighted = grad_rows * att_ref[0, start:seen, :] / den
        total_q = None
        for head in range(2):
            q_head, g_head = head_mask(queries, head), head_mask(unnorm, head)
            exp_scores = causal_exp(dot(q_head, keys, 1, 1), start)
            grad_total = -jnp.sum(head_mask(weighted, head), axis=1, keepdims=True)
            grad_scores = (exp_scores * (dot(g_head, values, 1, 1) + grad_total)).astype(BF)
            part = dot(grad_scores, head_mask(keys, head), 1, 0)
            total_q = part if total_q is None else total_q + part
            grad_k[:seen, :] += dot(grad_scores, q_head, 0, 0)
            grad_v[:seen, :] += dot(exp_scores.astype(BF), g_head, 0, 0)
        grad_q[start:seen, :] = total_q * 0.125
    for block in range(length // BLK):
        slot = me ^ block
        rows = slice(block * BLK, (block + 1) * BLK)
        cos_rows, sin_rows = cosine[rows, :], sine[rows, :]
        for part, held in enumerate((grad_q, grad_k)):
            value = held[rows, :]
            raw = value * cos_rows + turn(value * sin_rows, True)
            out[chunk_of(slot), slot & 1, 0, :, part * 128 : (part + 1) * 128] = raw.astype(BF)
        out[chunk_of(slot), slot & 1, 0, :, 256:] = grad_v[rows, :].astype(BF)


def whole(shape):
    return pl.BlockSpec(shape, lambda i, place: (0,) * len(shape))


def per_seq(shape, at):
    return pl.BlockSpec(shape, lambda i, place: tuple(i if d == at else 0 for d in range(len(shape))))


def attend(place, proj, cosine, sine):
    length = cosine.shape[0]
    seq = jax.ShapeDtypeStruct((2, length, 128), BF)
    wide = jax.ShapeDtypeStruct((2, length, 128), F32)
    return pl.pallas_call(
        attend_kernel,
        grid_spec=pltpu.PrefetchScalarGridSpec(
            num_scalar_prefetch=1,
            grid=(2,),
            in_specs=[per_seq((4, 2, 1, BLK, 384), 2), whole((length, 128)), whole((length, 128))],
            out_specs=[per_seq((1, length, 128), 0)] * 5 + [per_seq((4, 2, 1, BLK, 128), 2)],
        ),
        out_shape=[seq, seq, seq, wide, wide, jax.ShapeDtypeStruct((4, 2, 2, BLK, 128), BF)],
        compiler_params=pltpu.CompilerParams(vmem_limit_bytes=40 << 20),
        cost_estimate=pl.CostEstimate(flops=0, bytes_accessed=1 << 20, transcendentals=0),
        name="attend",
    )(place, proj, cosine, sine)


def attend_back(place, saved, grad_slots, cosine, sine):
    length = cosine.shape[0]
    return pl.pallas_call(
        attend_back_kernel,
        grid_spec=pltpu.PrefetchScalarGridSpec(
            num_scalar_prefetch=1,
            grid=(2,),
            in_specs=[per_seq((1, length, 128), 0)] * 5
            + [per_seq((4, 2, 1, BLK, 128), 2), whole((length, 128)), whole((length, 128))],
            out_specs=per_seq((4, 2, 1, BLK, 384), 2),
            scratch_shapes=[pltpu.VMEM((length, 128), F32)] * 4,
        ),
        out_shape=jax.ShapeDtypeStruct((4, 2, 2, BLK, 384), BF),
        compiler_params=pltpu.CompilerParams(vmem_limit_bytes=40 << 20),
        cost_estimate=pl.CostEstimate(flops=0, bytes_accessed=1 << 20, transcendentals=0),
        name="attend_back",
    )(place, *saved, grad_slots, cosine, sine)


def perm_of(target):
    pairs = []
    for index in range(32):
        bits = [(index >> shift) & 1 for shift in (4, 3, 2, 1, 0)]
        place = 0
        for bit in target(*bits):
            place = 2 * place + bit
        pairs.append((index, place))
    return pairs


def join_kernel(place, pair, far, pair_c, far_c, out):
    cols = pair.shape[1]
    early = pl.program_id(0) < 2
    for core in range(2):
        here, there = slice(core * cols, (core + 1) * cols), slice((1 - core) * cols, (2 - core) * cols)

        @pl.when((place[3] == core) & early)
        def _():
            out[:, here] = pair[...]
            out[:, there] = pair_c[...]

        @pl.when((place[3] == core) & jnp.logical_not(early))
        def _():
            out[:, here] = far[...]
            out[:, there] = far_c[...]


def join_out(place, pair, far, pair_c, far_c):
    rows, cols = pair.shape[0] // 2, pair.shape[1]
    early = pl.BlockSpec((rows, cols), lambda i, place: (jnp.minimum(i, 1), 0))
    late = pl.BlockSpec((rows, cols), lambda i, place: (jnp.maximum(i - 2, 0), 0))
    return pl.pallas_call(
        join_kernel,
        grid_spec=pltpu.PrefetchScalarGridSpec(
            num_scalar_prefetch=1,
            grid=(4,),
            in_specs=[early, late, early, late],
            out_specs=pl.BlockSpec(
                (rows, 2 * cols), lambda i, place: (place[2] ^ (((i & 1) << 1) | (i >> 1)), 0)
            ),
        ),
        out_shape=jax.ShapeDtypeStruct((4 * rows, 2 * cols), BF),
        cost_estimate=pl.CostEstimate(flops=0, bytes_accessed=1 << 20, transcendentals=0),
        name="join_out",
    )(place, pair, far, pair_c, far_c)


def order_kernel(place, block, out):
    out[...] = block[...]


def order_rows(place, value):
    rows, cols = value.shape[0] // 4, value.shape[1]
    return pl.pallas_call(
        order_kernel,
        grid_spec=pltpu.PrefetchScalarGridSpec(
            num_scalar_prefetch=1,
            grid=(4,),
            in_specs=[pl.BlockSpec((rows, cols), lambda i, place: (i, 0))],
            out_specs=pl.BlockSpec((rows, cols), lambda i, place: (place[2] ^ i, 0)),
        ),
        out_shape=jax.ShapeDtypeStruct(value.shape, BF),
        cost_estimate=pl.CostEstimate(flops=0, bytes_accessed=1 << 20, transcendentals=0),
        name="order_rows",
    )(place, value)


def slot_of(rel):
    bit_y, bit_z0, bit_c, bit_z1 = rel >> 3, (rel >> 2) & 1, (rel >> 1) & 1, rel & 1
    return ORDER.index(2 * bit_z1 + bit_z0) * 4 + bit_c * 2 + bit_y


def to_heads_kernel(place, slots, out):
    for rel in range(16):
        pair = place[1] ^ rel
        out[:, pl.ds(pl.multiple_of(pair * 128, 128), 128)] = slots[slot_of(rel)]


def to_slots_kernel(place, rows, out):
    for rel in range(16):
        pair = place[1] ^ rel
        out[slot_of(rel)] = rows[:, pl.ds(pl.multiple_of(pair * 128, 128), 128)]


def reorder(kernel, place, value, shape):
    return pl.pallas_call(
        kernel,
        in_specs=[pl.BlockSpec(memory_space=pltpu.SMEM), pl.BlockSpec(memory_space=pltpu.VMEM)],
        out_specs=pl.BlockSpec(memory_space=pltpu.VMEM),
        out_shape=jax.ShapeDtypeStruct(shape, BF),
        cost_estimate=pl.CostEstimate(flops=0, bytes_accessed=1 << 20, transcendentals=0),
        name=kernel.__name__,
    )(place, value)


def split(value, dim, bit):
    size = value.shape[dim] // 2
    return (
        lax.dynamic_slice_in_dim(value, bit * size, size, dim),
        lax.dynamic_slice_in_dim(value, (1 - bit) * size, size, dim),
    )


def ff_place(at_y, at_x, at_z1, at_z0, at_c):
    return at_y, at_z0, at_z1, at_x, at_c


def attn_place(at_y, at_x, at_z1, at_z0, at_c):
    return at_z1, at_x, at_y, at_z0, at_c


def move(value, target):
    return lax.ppermute(value.astype(BF), AXES, perm_of(target)).astype(F32)


def ff_step(value, name, leaving):
    flip = 8 if name == "x" else 2
    pairs = [(i, i ^ flip) for i in range(32) if (((i >> 3) ^ (i >> 1)) & 1) == leaving]
    return lax.ppermute(value, AXES, pairs)


def body(residual_in, attn_gain, mlp_gain, w_qkv, w_out, w_gate_up, w_down, cotangent):
    y, x, z, c = [lax.axis_index(name) for name in AXES]
    z1, z0 = z >> 1, z & 1
    group, part = 2 * y + x, 2 * z + c
    width = residual_in.shape[2]
    length = BLK * 8
    quarter = 4 * BLK
    units = w_gate_up.shape[0] // 8
    inputs = residual_in[0].astype(F32)
    gain_one, gain_two = attn_gain.astype(F32), mlp_gain.astype(F32)
    scale_one = rms_scale(inputs)
    normed_one = (inputs * scale_one * gain_one).astype(BF)

    qkv_sent = lax.dynamic_slice_in_dim(w_qkv, (4 * c + 2 * z1) * HD, 2 * HD, 0)
    qkv_sent = jnp.transpose(qkv_sent, (1, 0, 2)).reshape(3 * 2 * HD, width)
    x_pairs = [((i & 1) * 4 + i, (1 - (i & 1)) * 4 + i) for i in range(4)]
    y_pairs = [((i >> 1) * 4 + i, (1 - (i >> 1)) * 4 + i) for i in range(4)]
    hops = [normed_one] + [hop(normed_one, j) for j in ORDER[1:]]
    others = [swap(normed_one, "y")]
    qkv_moved = lax.ppermute(qkv_sent, ("x", "z"), x_pairs)
    cols = width // 2
    out_own = lax.dynamic_slice_in_dim(w_out, c * cols, cols, 1)
    hops[3], qkv_moved = tick(hops[3], qkv_moved)
    others += [swap(held, "y") for held in hops[1:]]
    normed_all = jnp.concatenate([with_partner(*item) for item in zip(hops, others)], axis=0)
    heads_qkv = jnp.where(x == z0, qkv_sent, qkv_moved)

    def columns(side):
        first = (8 * (2 * z1 + side) + 4 * c + z0) * units
        return jnp.concatenate(
            [lax.dynamic_slice_in_dim(w_down, first + 2 * j * units, units, 1) for j in range(2)], axis=1
        )

    gu_sent = [lax.dynamic_slice_in_dim(w_gate_up, (4 * c + 2 * j + z0) * units, units, 0) for j in range(2)]
    gate_sent = [jnp.reshape(item[:, 0], (units, width)) for item in gu_sent]
    up_sent = [jnp.reshape(item[:, 1], (units, width)) for item in gu_sent]
    down_own, down_sent = columns(x), columns(1 - x)

    def to_y(value):
        return lax.ppermute(value, ("y", "z"), y_pairs)

    cos_half, sin_half = rope_tables(jnp.arange(length, dtype=jnp.int32), HD // 2)
    cosine, sine = jnp.tile(cos_half, (1, 4)), jnp.tile(sin_half, (1, 4))
    place = jnp.stack([part, 8 * y + 4 * z0 + 2 * c + z1, group, c]).astype(jnp.int32)

    *firsts, cot, out_own, down_sent, down_own = tick(
        normed_all, heads_qkv, *gate_sent, *up_sent, cosine, sine, place, cotangent[0], out_own, down_sent, down_own
    )
    normed_all, heads_qkv, gate_sent, up_sent = firsts[0], firsts[1], firsts[2:4], firsts[4:6]
    cosine, sine, place = firsts[6:]
    cot_hops = [cot, hop(cot, 1), hop(cot, 3), None]
    cot_others = [swap(cot, "x")]
    down_x = swap(down_sent, "x")
    out_y = swap(out_own, "y")

    proj = dot(normed_all, heads_qkv, 1, 1)
    *saved, low_slots = attend(place, proj.reshape(4, 2, 2, BLK, 384), cosine, sine)
    pieces = send_core(low_slots)
    pieces, out_y, cot_hops[1], cot_others[0], down_x = tick(pieces, out_y, cot_hops[1], cot_others[0], down_x)
    out_pair = jnp.concatenate([out_own, out_y], axis=0)
    out_x = swap(out_pair, "x")
    down_pair = jnp.concatenate([down_own, down_x], axis=0)
    down_y = swap(down_pair, "y")
    pair_c = swap(out_pair, "c")
    pieces = send_plane(pieces, "y")
    pieces, cot_hops[2] = tick(pieces, cot_hops[2])
    pieces = send_hops(pieces)
    pieces, out_x, down_y, gate_sent[0], cot, pair_c = tick(pieces, out_x, down_y, gate_sent[0], cot, pair_c)
    cot_hops[3] = hop(cot, 2)
    gate_moved = [to_y(gate_sent[0])]
    attended = reorder(to_heads_kernel, place, pieces.reshape(16, BLK, 128), (BLK, width))
    out_full = join_out(place, out_pair, out_x, pair_c, swap(out_x, "c"))
    attended, out_full, cot_hops[1], cot_hops[2] = tick(attended, out_full, cot_hops[1], cot_hops[2])
    cot_others += [swap(item, "x") for item in cot_hops[1:3]]
    residual = inputs + dot(attended, out_full, 1, 1)
    scale_two = rms_scale(residual)
    normed_two = (residual * scale_two * gain_two).astype(BF)

    normed_two, cot_hops[3], gate_moved[0], gate_sent[1], down_pair, down_y, cot_hops[0], cot_others[0] = tick(
        normed_two, cot_hops[3], gate_moved[0], gate_sent[1], down_pair, down_y, cot_hops[0], cot_others[0]
    )
    gate_moved.append(to_y(gate_sent[1]))
    hops = [normed_two] + [hop(normed_two, j) for j in ORDER[1:]]
    others = [swap(normed_two, "x")]
    hops[1], gate_moved[1], up_sent[0], cot_others[1] = tick(hops[1], gate_moved[1], up_sent[0], cot_others[1])
    up_moved = [to_y(up_sent[0])]
    others.append(swap(hops[1], "x"))
    hops[2], up_moved[0], up_sent[1], cot_others[2], cot_hops[3] = tick(
        hops[2], up_moved[0], up_sent[1], cot_others[2], cot_hops[3]
    )
    up_moved.append(to_y(up_sent[1]))
    others.append(swap(hops[2], "x"))
    cot_others.append(swap(cot_hops[3], "x"))
    others.append(swap(hops[3], "x"))
    w_gate, w_up = [
        jnp.concatenate([jnp.where(y == z1, own, moved) for own, moved in zip(held, arrived)], axis=0)
        for held, arrived in ((gate_sent, gate_moved), (up_sent, up_moved))
    ]
    down = order_rows(place, jnp.concatenate([down_pair, down_y], axis=0))
    ff_chunks = [with_partner(*item) for item in zip(hops, others)]
    cot_chunks = [with_partner(*item) for item in zip(cot_hops, cot_others)]

    hiddens, gate_grads, up_grads, back_parts, mlp_parts = [[None] * 4 for _ in range(5)]
    first, second, third, last = turns = (2, 3, 1, 0)
    for i in turns:
        if i == third:
            ff_chunks[i], back_parts[first] = tick(ff_chunks[i], back_parts[first])
            back_parts[first] = fold_plane(back_parts[first], "x")
        if i == last:
            ff_chunks[i], back_parts[second], back_parts[first], mlp_parts[first] = tick(
                ff_chunks[i], back_parts[second], back_parts[first], mlp_parts[first]
            )
            mlp_parts[first] = fold_plane(mlp_parts[first], "x")
            back_parts[second] = fold_plane(back_parts[second], "x")
        gate, up = dot(ff_chunks[i], w_gate, 1, 1), dot(ff_chunks[i], w_up, 1, 1)
        sigmoid_gate = jax.nn.sigmoid(gate)
        silu = gate * sigmoid_gate
        hidden = (silu * up).astype(BF)
        grad_hidden = dot(cot_chunks[i], down, 1, 0)
        grad_gate = (grad_hidden * up * sigmoid_gate * (1.0 + gate * (1.0 - sigmoid_gate))).astype(BF)
        grad_up = (grad_hidden * silu).astype(BF)
        back_parts[i] = dot(grad_gate, w_gate, 1, 0) + dot(grad_up, w_up, 1, 0)
        if i == last:
            tied = tick(back_parts[i], *gate_grads[1:], *up_grads[1:], *hiddens[1:], grad_gate, grad_up, hidden)
            back_parts[i], gate_grads[1:], up_grads[1:], hiddens[1:] = tied[0], tied[1:4], tied[4:7], tied[7:10]
            grad_gate, grad_up, hidden = tied[10:]
        back_parts[i] = fold_core(back_parts[i])
        mlp_parts[i] = fold_core(dot(hidden, down, 1, 1))
        hiddens[i], gate_grads[i], up_grads[i] = hidden, grad_gate, grad_up

    def over_chunks(left, right):
        return sum(dot(left[i], right[i], 0, 0) for i in range(4)).astype(BF)

    back_hops = [None] * 4

    def send_back(i):
        back_hops[i] = hop(back_parts[i].astype(BF), ORDER[i])

    send_back(first)
    gate_grad = over_chunks(gate_grads, ff_chunks)
    gate_grad, *up_grads, back_parts[third], back_parts[second], mlp_parts[second], mlp_parts[first] = tick(
        gate_grad, *up_grads, back_parts[third], back_parts[second], mlp_parts[second], mlp_parts[first]
    )
    mlp_parts[second] = fold_plane(mlp_parts[second], "x")
    back_parts[third] = fold_plane(back_parts[third], "x")
    send_back(second)
    gate_own, gate_other = split(gate_grad, 0, y)
    gate_other = swap(gate_other, "y")
    up_grad = over_chunks(up_grads, ff_chunks)
    up_grad, *hiddens, back_parts[last], back_parts[third], mlp_parts[third], gate_other = tick(
        up_grad, *hiddens, back_parts[last], back_parts[third], mlp_parts[third], gate_other
    )
    mlp_parts[third] = fold_plane(mlp_parts[third], "x")
    back_parts[last] = fold_plane(back_parts[last], "x")
    send_back(third)
    up_own, up_other = split(up_grad, 0, y)
    up_other = swap(up_other, "y")
    down_grad = over_chunks(cot_chunks, hiddens)
    down_own, down_other = split(down_grad, 1, y)
    back_parts[last], down_other, mlp_parts[last], mlp_parts[second] = tick(
        back_parts[last], down_other, mlp_parts[last], mlp_parts[second]
    )
    mlp_parts[last] = fold_plane(mlp_parts[last], "x")
    mlp_hops = [None] + [hop(mlp_parts[i].astype(BF), ORDER[i]) for i in (1, 2, 3)]
    back_parts[last], *back_hops[1:], up_other, down_other = tick(
        back_parts[last], *back_hops[1:], up_other, down_other
    )
    down_other = swap(down_other, "y")
    grad_normed_two = back_parts[last] + back_hops[1] + back_hops[2] + back_hops[3]

    grad_norm_two, grad_gain_two = rms_back(grad_normed_two, residual, scale_two, gain_two)
    grad_residual = cotangent[0].astype(F32) + grad_norm_two
    grad_branch = grad_residual.astype(BF)
    grad_attended = dot(grad_branch, out_full, 1, 0).astype(BF)
    grad_slots = reorder(to_slots_kernel, place, grad_attended, (16, BLK, 128))
    pieces = send_hops(grad_slots.reshape(4, 2, 2, BLK, 128))
    pieces, mlp_hops[first], grad_branch, down_other, gate_other, up_other = tick(
        pieces, mlp_hops[first], grad_branch, down_other, gate_other, up_other
    )
    gate_sum = (gate_own.astype(F32) + gate_other.astype(F32)).astype(BF)
    up_sum = (up_own.astype(F32) + up_other.astype(F32)).astype(BF)
    gate_step, up_step = ff_step(gate_sum, "x", 1), ff_step(up_sum, "z", 1)
    branch_hops = [grad_branch] + [hop(grad_branch, j) for j in ORDER[1:]]
    pieces = send_core(send_plane(pieces, "y"))
    grad_proj = attend_back(place, saved, pieces, cosine, sine).reshape(16 * BLK, 384)
    back_parts = [fold_core(dot(grad_proj[j * quarter : (j + 1) * quarter], heads_qkv, 1, 0)) for j in range(4)]
    qkv_grad = dot(grad_proj, normed_all, 0, 0)
    qkv_own, qkv_other = split(qkv_grad.reshape(3, 2 * HD, width), 1, x)
    *back_parts, qkv_other, mlp_hops[second] = tick(*back_parts, qkv_other.astype(BF), mlp_hops[second])
    qkv_other = swap(qkv_other, "x")
    back_parts = [fold_plane(item, "y") for item in back_parts]
    down_sum = (down_own.astype(F32) + down_other.astype(F32)).astype(BF)
    half = down_sum.shape[0] // 2
    down_steps = [ff_step(down_sum[:half], "x", 1), ff_step(down_sum[half:], "z", 1)]
    back_parts[first], branch_hops[1], branch_hops[2] = tick(back_parts[first], branch_hops[1], branch_hops[2])
    send_back(first)
    back_parts[second], branch_hops[3], mlp_hops[third], gate_step, up_step = tick(
        back_parts[second], branch_hops[3], mlp_hops[third], gate_step, up_step
    )
    send_back(second)
    gate_step, up_step = ff_step(gate_step, "z", 0), ff_step(up_step, "x", 0)
    back_parts[third], back_parts[last], *branch_hops = tick(back_parts[third], back_parts[last], *branch_hops)
    send_back(third)
    branch_others = [swap(item, "y") for item in branch_hops]
    branch_others[0], back_hops[first], qkv_other, *down_steps = tick(
        branch_others[0], back_hops[first], qkv_other, *down_steps
    )
    down_steps = [ff_step(down_steps[0], "z", 0), ff_step(down_steps[1], "x", 0)]
    qkv_moved = lax.ppermute((qkv_own + qkv_other.astype(F32)).astype(BF), AXES, perm_of(attn_place))
    branch_others[2], back_hops[second], mlp_parts[last], qkv_grad, gate_step, up_step, qkv_moved = tick(
        branch_others[2], back_hops[second], mlp_parts[last], qkv_grad, gate_step, up_step, qkv_moved
    )
    branch_chunks = [with_partner(*item) for item in zip(branch_hops, branch_others)]
    mlp_term = mlp_parts[last] + sum(item.astype(F32) for item in mlp_hops[1:])
    layer_out = (residual + mlp_term).astype(BF)
    gain_part = jnp.sum(qkv_grad * heads_qkv.astype(F32), axis=0) / gain_one
    low_chunks = low_slots.reshape(4, quarter, 128)
    out_grad = sum(dot(item, low_chunks[i], 0, 0) for i, item in enumerate(branch_chunks))
    out_own, out_other = split(out_grad, 1, x)
    grad_out_proj = move(out_own + swap(out_other.astype(BF), "x").astype(F32), attn_place)
    grad_normed_one = back_parts[last] + back_hops[1] + back_hops[2] + back_hops[3]
    grad_qkv = jnp.transpose(qkv_moved.astype(F32), (1, 0, 2))
    stays = x == z0
    grad_gate_up = jnp.stack([jnp.where(stays, gate_sum, gate_step), jnp.where(stays, up_sum, up_step)], axis=1).astype(F32)
    grad_down = jnp.where(stays, down_sum, jnp.concatenate(down_steps, axis=0)).astype(F32)

    weighted = grad_normed_one * gain_one
    inner_mean = jnp.mean(weighted * inputs, axis=-1, keepdims=True)
    grad_input = grad_residual + scale_one * weighted - inputs * scale_one**3 * inner_mean

    gains = jnp.stack([gain_part, grad_gain_two])
    for name, bit in (("y", y), ("x", x)):
        mine, other = split(gains, 1, bit)
        gains = mine + swap(other, name)
    size = gains.shape[1] // 4
    quarters = [lax.dynamic_slice_in_dim(gains, (z ^ j) * size, size, 1) for j in range(4)]
    gains = quarters[0] + hop(quarters[1], 1) + hop(quarters[2], 2) + hop(quarters[3], 3)
    mine, other = split(gains, 1, c)
    gains = mine + swap(other, "c")
    return (
        layer_out[None],
        grad_input[None],
        gains[0],
        gains[1],
        grad_qkv,
        grad_out_proj,
        grad_gate_up,
        grad_down,
    )


def solution(mesh):
    if mesh.shape["fsdp"] != 4 or mesh.shape["seq"] != 8:
        return general_solution(mesh)
    fine = Mesh(mesh.devices.reshape(2, 2, 4, 2), AXES)
    fsdp, seq = ("y", "x"), ("z", "c")
    tokens = P(fsdp, seq, None)
    return jax.shard_map(
        body,
        mesh=fine,
        in_specs=(
            tokens,
            P(),
            P(),
            P(fsdp, None, None),
            P(fsdp, None),
            P(fsdp, None, None),
            P(fsdp, None),
            tokens,
        ),
        out_specs=(
            tokens,
            tokens,
            P(fsdp + seq),
            P(fsdp + seq),
            P(seq + fsdp, None, None),
            P(None, seq + fsdp),
            P(seq + fsdp, None, None),
            P(None, seq + fsdp),
        ),
        check_vma=False,
    )
```
